128 devices in a mesh: dp: 32 (over z, x, core), mp: 4 (over y).
Axes of the slice: x: 4, y: 4, z: 4, core: 2. Of those that a mesh axis runs over, the one named last changes fastest.
Arguments:
- features: bfloat16 [4096, 32, 512], P(('dp', 'mp')), may hold values from -6 to 6
- lengths: int32 [4096], P(('dp', 'mp')), may hold values from 1 to 7, as said below
- dests: int32 [4096], P(('dp', 'mp')), may hold values from 0 to 31, as said below
- offsets: int32 [4096], P(('dp', 'mp')), may hold values from 0 to 511, as said below
- conv_weight: bfloat16 [2, 1024, 512], replicated, may hold values from -0.1875 to 0.1875
- norm_gain: float32 [2, 512], replicated, may hold values from 0.1 to 1.9
- norm_shift: float32 [2, 512], replicated, may hold values from -3 to 3
- proj_weight: bfloat16 [512, 1280], P(None, 'mp'), may hold values from -0.25 to 0.25
- grad_packed: bfloat16 [16384, 1280], P('dp', 'mp'), may hold values from -6 to 6
Outputs:
- packed: bfloat16 [16384, 1280], P('dp', 'mp')
- grad_features: bfloat16 [4096, 32, 512], P(('dp', 'mp'))
- grad_conv: float32 [2, 1024, 512], P(None, ('dp', 'mp'))
- grad_norm: float32 [2, 1024], P(None, ('dp', 'mp'))
- grad_proj: float32 [512, 1280], P('dp', 'mp')
The draws below stay inside these ranges and needn't reach their ends.
Inputs may be any that keep to these rules, and one draw needn't show every extreme that they name: Utterances 2k and 2k+1 of each device form a pair whose lengths sum to 8. `dests`: both utterances of a pair name the same shard; the 16 pairs of one device name different shards, and every shard is named by exactly 64 pairs. A pair fills one aligned block of 8 rows of its shard that no other pair uses: the first utterance starts at offsets[2k], a multiple of 8, and the second at offsets[2k] + lengths[2k].
All inputs are finite; a program needn't handle non-finite values.
Results may differ from the reference program's by a relative error of at most 0.015.
Values may be sent and summed in bfloat16 or wider, within the bound.
A program may use at most 64 MiB of HBM per device.

```python
import jax
import jax.numpy as jnp
from jax import lax

C = 512
HID = 1280
LAYERS = 2
FU = 8
GROUPS = 16
UTT_DEV = 32
BLOCKS = 64
ROWS = 512
UTTS = 4096
SEQ_ROWS = 16384


def pair_plan(key):
    dp_total = 2 * GROUPS
    device_total = UTTS // UTT_DEV
    mp_total = device_total // dp_total
    shuffled = jax.random.permutation(jax.random.fold_in(key, 101), device_total).astype(jnp.int32)
    base_shard = shuffled // mp_total
    within = shuffled % mp_total
    rotations = jax.random.permutation(jax.random.fold_in(key, 102), dp_total)[:GROUPS].astype(jnp.int32)
    pair_dest = (base_shard[:, None] + rotations[None, :]) % dp_total
    natural = jnp.arange(GROUPS, dtype=jnp.int32)[None, :] * mp_total + within[:, None]
    shard_keys = jax.random.split(jax.random.fold_in(key, 103), dp_total)
    shuffles = jax.vmap(lambda one_key: jax.random.permutation(one_key, BLOCKS))(shard_keys).astype(jnp.int32)
    pair_block = shuffles[pair_dest, natural]
    first_len = jax.random.randint(jax.random.fold_in(key, 104), (device_total, GROUPS), 1, FU, dtype=jnp.int32)
    last_pair = jnp.logical_and(pair_dest == 0, pair_block == BLOCKS - 1)
    first_len = jnp.where(last_pair, FU - 1, first_len).astype(jnp.int32)
    lengths = jnp.stack([first_len, FU - first_len], axis=-1).reshape(UTTS).astype(jnp.int32)
    dests = jnp.stack([pair_dest, pair_dest], axis=-1).reshape(UTTS).astype(jnp.int32)
    block_start = pair_block * FU
    offsets = jnp.stack([block_start, block_start + first_len], axis=-1).reshape(UTTS).astype(jnp.int32)
    return (lengths, dests, offsets)


def draw_lengths(key, part):
    return pair_plan(key)[0]


def draw_dests(key, part):
    return pair_plan(key)[1]


def draw_offsets(key, part):
    return pair_plan(key)[2]


def level_of(rng, dims, cuts, smallest, largest):
    gain = 1.0
    for axis_at, shards_of in cuts:
        draws = jax.random.uniform(jax.random.fold_in(jax.random.fold_in(rng, 6), axis_at), (shards_of,), jnp.float32, smallest / len(cuts), largest / len(cuts))
        gain = gain * jnp.repeat(jnp.exp(draws), dims[axis_at] // shards_of).reshape((-1,) + (1,) * (len(dims) - 1 - axis_at))
    return gain


def normal_values(rng, shape, scale, limit, cuts=(), kind=jnp.bfloat16):
    entries = scale * jax.random.normal(rng, shape, jnp.float32)
    if cuts:
        entries = entries * level_of(rng, shape, cuts, -0.22, 0.18)
    return jnp.clip(entries, -limit, limit).astype(kind)


def setup_inputs(seed: int = 0) -> dict:
    splits = jax.random.split(jax.random.key(seed), 10)
    features = normal_values(splits[0], (UTTS, 4 * FU, C), 1.0, 6.0, ((0, 128),))
    lengths = draw_lengths(jax.random.fold_in(splits[9], 71), 0)
    dests = draw_dests(jax.random.fold_in(splits[9], 71), 0)
    offsets = draw_offsets(jax.random.fold_in(splits[9], 71), 0)
    conv_weight = normal_values(splits[4], (LAYERS, 2 * C, C), (2 * C) ** -0.5, 0.1875)
    norm_gain = jnp.clip(1.0 + 0.18 * jax.random.normal(splits[5], (LAYERS, C), jnp.float32), 0.1, 1.9)
    norm_shift = normal_values(splits[6], (LAYERS, C), 0.5, 3.0, (), jnp.float32)
    proj_weight = normal_values(splits[7], (C, HID), C ** -0.5, 0.25, ((1, 4),))
    grad_packed = normal_values(splits[8], (SEQ_ROWS, HID), 1.0, 6.0, ((0, 32), (1, 4)))
    return {"features": features, "lengths": lengths, "dests": dests, "offsets": offsets, "conv_weight": conv_weight, "norm_gain": norm_gain, "norm_shift": norm_shift, "proj_weight": proj_weight, "grad_packed": grad_packed}


epsilon = 1e-05

def norm_gelu(pre_norm, gain_row, shift_row):
    average = lax.optimization_barrier(jnp.mean(pre_norm, axis=-1, keepdims=True))
    centred = pre_norm - average
    spread = lax.optimization_barrier(jnp.mean(centred * centred, axis=-1, keepdims=True))
    return jax.nn.gelu(centred * lax.rsqrt(spread + epsilon) * gain_row + shift_row, approximate=False)

def encode_block(inputs, conv_weight, norm_gain, norm_shift):
    channels = inputs.shape[-1]
    first_in = inputs.reshape(-1, 2 * channels)
    first_out = jnp.dot(first_in, conv_weight[0], preferred_element_type=jnp.float32)
    hidden = norm_gelu(first_out, norm_gain[0], norm_shift[0]).astype(jnp.bfloat16)
    second_in = hidden.reshape(-1, 2 * channels)
    second = jnp.dot(second_in, conv_weight[1], preferred_element_type=jnp.float32)
    frames = norm_gelu(second, norm_gain[1], norm_shift[1]).astype(jnp.bfloat16)
    return (first_in, first_out, second_in, second, frames)

def back_block(inputs, grad_frames, conv_weight, norm_gain, norm_shift):
    channels = inputs.shape[-1]
    first_in, first_out, second_in, second, frames = encode_block(inputs, conv_weight, norm_gain, norm_shift)
    unused_second, pull_second = jax.vjp(norm_gelu, second, norm_gain[1], norm_shift[1])
    grad_second, gain_second, shift_second = pull_second(lax.optimization_barrier(grad_frames).astype(jnp.float32))
    grad_second = grad_second.astype(jnp.bfloat16)
    grad_hidden = jnp.dot(grad_second, conv_weight[1].T, preferred_element_type=jnp.float32).astype(jnp.bfloat16)
    grad_hidden = lax.optimization_barrier(grad_hidden).reshape(-1, channels).astype(jnp.float32)
    unused_first, pull_first = jax.vjp(norm_gelu, first_out, norm_gain[0], norm_shift[0])
    grad_first, gain_first, shift_first = pull_first(grad_hidden)
    grad_first = grad_first.astype(jnp.bfloat16)
    grad_inputs = jnp.dot(grad_first, conv_weight[0].T, preferred_element_type=jnp.float32).astype(jnp.bfloat16)
    grad_weight = jnp.stack([jnp.dot(first_in.T, grad_first, preferred_element_type=jnp.float32), jnp.dot(second_in.T, grad_second, preferred_element_type=jnp.float32)])
    grad_norms = jnp.stack([jnp.concatenate([gain_first, shift_first]), jnp.concatenate([gain_second, shift_second])])
    return (grad_inputs.reshape(inputs.shape), grad_weight, grad_norms)

def reference(features, lengths, dests, offsets, conv_weight, norm_gain, norm_shift, proj_weight, grad_packed):
    device_total = UTTS // UTT_DEV
    blocks_in = features.reshape(device_total, UTT_DEV * 4 * FU, C)

    def forward_one(device_block):
        return encode_block(device_block, conv_weight, norm_gain, norm_shift)[4]
    frames = lax.map(forward_one, blocks_in).reshape(UTTS, FU, C)
    frame_index = jnp.arange(FU, dtype=jnp.int32)
    is_live = frame_index[None, :] < lengths[:, None]
    row_index = jnp.where(is_live, dests[:, None] * ROWS + offsets[:, None] + frame_index[None, :], SEQ_ROWS)
    row_index = row_index.astype(jnp.int32).reshape(-1)
    packed_in = jnp.zeros((SEQ_ROWS, C), jnp.bfloat16).at[row_index].set(frames.reshape(-1, C), mode='drop')
    packed = jnp.dot(packed_in, proj_weight, preferred_element_type=jnp.float32).astype(jnp.bfloat16)
    grad_proj = jnp.dot(packed_in.T, grad_packed, preferred_element_type=jnp.float32)
    grad_rows = jnp.dot(grad_packed, proj_weight.T, preferred_element_type=jnp.float32).astype(jnp.bfloat16)
    padded_rows = jnp.concatenate([grad_rows, jnp.zeros((1, C), jnp.bfloat16)], axis=0)
    grad_frames = padded_rows[row_index].reshape(device_total, UTT_DEV * FU, C)

    def back_one(totals, pieces):
        device_block, grad_block = pieces
        grad_inputs, grad_weight, grad_norms = back_block(device_block, grad_block, conv_weight, norm_gain, norm_shift)
        return ((totals[0] + grad_weight, totals[1] + grad_norms), grad_inputs)
    zero_sums = (jnp.zeros((LAYERS, 2 * C, C), jnp.float32), jnp.zeros((LAYERS, 2 * C), jnp.float32))
    sums, grad_features = lax.scan(back_one, zero_sums, (blocks_in, grad_frames))
    grad_features = grad_features.reshape(UTTS, 4 * FU, C)
    return (packed, grad_features, sums[0], sums[1], grad_proj)
```

```python
import jax
import jax.numpy as jnp
from jax import lax
from jax.experimental import pallas as pl
from jax.experimental.pallas import tpu as pltpu
from jax.sharding import PartitionSpec as P

EPSILON = 1e-05
BF = jnp.bfloat16
F32 = jnp.float32
MESH = pl.DeviceIdType.MESH
NN = (((1,), (0,)), ((), ()))
NT = (((1,), (1,)), ((), ()))
TN = (((0,), (0,)), ((), ()))
LANE = 128


def dot(a, b, dims=NN):
    return lax.dot_general(a, b, dims, preferred_element_type=F32)


def iota(shape, dim):
    return lax.broadcasted_iota(jnp.int32, shape, dim)


def kernel(
    idx_ref, tgt_ref, gain_ref, shift_ref, feat_hbm, weight_hbm, proj_hbm, gp_hbm,
    packed_out, gfeat_out, gconv_out, gproj_out, gnorm_out,
    xb, wv, gpv, xf, act, pre, xhat0, der0, rstd0, xhat1, der1, rstd1, hid, frm, slots,
    tbl, query, gsend, grecv, psend, precv, pall, packv,
    gh, gf, gx, xo, gfv,
    convp, convr, convb, conv1, convb1, conv2, convb2, conv3,
    projp, projr, projb, proj1, projb1, proj2, projb2, proj3,
    nrm, nrmr, nrm1,
    in_sem, out_sem, idx_s, idx_r, ag_s, ag_r, a2a_s, a2a_r, rs_s, rs_r, nm_s, nm_r,
):
    dp = lax.axis_index("dp")
    y = lax.axis_index("mp")
    z, q = dp // 8, dp % 8
    x, c = q // 2, q % 2
    d = dp * 4 + y

    def dp_of(zz, xx, cc):
        return zz * 8 + xx * 2 + cc

    def remote(src, dst, ssem, rsem, to):
        return pltpu.make_async_remote_copy(
            src_ref=src, dst_ref=dst, send_sem=ssem, recv_sem=rsem, device_id=to, device_id_type=MESH
        )

    def await_bytes(ref, sem):
        pltpu.make_async_copy(ref, ref, sem).wait()

    loads = [
        pltpu.make_async_copy(feat_hbm, xb, in_sem.at[0]),
        pltpu.make_async_copy(weight_hbm, wv, in_sem.at[1]),
        pltpu.make_async_copy(proj_hbm, pall.at[y], in_sem.at[2]),
        pltpu.make_async_copy(gp_hbm, gpv, in_sem.at[3]),
    ]
    for one in (2, 0, 1, 3):
        loads[one].start()

    partners = (
        [(dp, (y + k) % 4) for k in range(1, 4)]
        + [(z * 8 + (q + k) % 8, y) for k in range(1, 8)]
        + [(((z + k) % 4) * 8 + q, y) for k in range(1, 4)]
    )
    barrier = pltpu.get_barrier_semaphore()
    for to in partners:
        pl.semaphore_signal(barrier, inc=1, device_id=to, device_id_type=MESH)
    tbl[z, q, y] = idx_ref[...]
    pl.semaphore_wait(barrier, len(partners))

    sends = []

    def launch(copy):
        copy.start()
        sends.append(copy)

    for k in range(1, 4):
        launch(remote(tbl.at[z, q, y], tbl.at[z, q, y], idx_s.at[k - 1], idx_r.at[0], (dp, (y + k) % 4)))
    loads[2].wait()
    up, down, far = (y + 1) % 4, (y + 3) % 4, (y + 2) % 4
    launch(remote(pall.at[y, c], pall.at[y, c], ag_s.at[0], ag_r.at[0], (dp, up)))
    launch(remote(pall.at[y, c], pall.at[y, c], ag_s.at[1], ag_r.at[1], (dp, down)))

    loads[0].wait()

    @pl.loop(0, 8)
    def _(i):
        rows = xb[pl.ds(pl.multiple_of(i * 128, 128), 128), :].astype(F32)
        for j in range(4):
            xf[j] = rows[:, j * LANE : (j + 1) * LANE]
        for k in range(4):
            part = jnp.concatenate([xf[j, pl.ds(k, 32, stride=4), :] for j in range(4)], axis=1)
            act[pl.ds(pl.multiple_of((k // 2) * 256 + i * 32, 32), 32), (k % 2) * 512 : (k % 2) * 512 + 512] = part.astype(BF)

    await_bytes(tbl.at[z, q, pl.ds(0, 3)], idx_r.at[0])
    for k in range(1, 8):
        launch(remote(tbl.at[z, q], tbl.at[z, q], idx_s.at[2 + k], idx_r.at[1], (z * 8 + (q + k) % 8, y)))

    loads[1].wait()
    pre[...] = dot(act[...], wv[0])

    await_bytes(pall.at[down, c], ag_r.at[0])
    launch(remote(pall.at[down, c, pl.ds(0, 128)], pall.at[down, c, pl.ds(0, 128)], ag_s.at[2], ag_r.at[2], (dp, up)))
    await_bytes(pall.at[up, c], ag_r.at[1])
    launch(remote(pall.at[up, c, pl.ds(128, 128)], pall.at[up, c, pl.ds(128, 128)], ag_s.at[3], ag_r.at[3], (dp, down)))

    await_bytes(tbl.at[z, pl.ds(0, 7)], idx_r.at[1])
    for k in range(1, 4):
        launch(remote(tbl.at[z], tbl.at[z], idx_s.at[9 + k], idx_r.at[2], (((z + k) % 4) * 8 + q, y)))

    def norm_gelu(source, gain, shift, xhat, der, rstd, start, count):
        v = source[pl.ds(start, count), :]
        mean = jnp.mean(v, axis=-1, keepdims=True)
        centred = v - mean
        spread = jnp.mean(centred * centred, axis=-1, keepdims=True)
        inv = lax.rsqrt(spread + EPSILON)
        normal = centred * inv
        arg = normal * gain + shift
        cdf = 0.5 + 0.5 * lax.erf(arg * (2.0**-0.5))
        xhat[pl.ds(start, count), :] = normal
        der[pl.ds(start, count), :] = cdf + arg * (jnp.exp(-0.5 * arg * arg) * 0.3989422804014327)
        rstd[pl.ds(start, count), :] = jnp.broadcast_to(inv, (count, LANE))
        return arg * cdf

    gain0, shift0 = gain_ref[0:1, :], shift_ref[0:1, :]
    gain1, shift1 = gain_ref[1:2, :], shift_ref[1:2, :]

    def first_rows(lo, hi):
        @pl.loop(lo, hi)
        def _(i):
            start = pl.multiple_of(i * 32, 32)
            for h in range(2):
                out = norm_gelu(pre, gain0, shift0, xhat0, der0, rstd0, pl.multiple_of(start + h * 256, 32), 32)
                hid[pl.ds(start, 32), h * 512 : (h + 1) * 512] = out.astype(BF)

    first_rows(0, 4)

    await_bytes(tbl.at[pl.ds(0, 3)], idx_r.at[2])
    table = tbl[...].reshape(128, LANE).astype(BF)
    pick = (iota((128, 512), 0) == dp).astype(F32).astype(BF)
    spread_s = ((iota((1024, 128), 0) >> 3) == iota((1024, 128), 1)).astype(F32).astype(BF)
    wanted = dot(spread_s, dot(table, pick).astype(BF))
    r_id = (iota((1024, 512), 0) & 7).astype(F32)
    c_id = iota((1024, 512), 1).astype(F32)
    one_hot = (wanted * 8.0 + r_id == c_id).astype(F32).astype(BF)
    loads[3].wait()
    gsend[...] = dot(one_hot, gpv[...]).astype(BF).reshape(128, 8, 320)

    own_g = pltpu.make_async_copy(gsend.at[d], grecv.at[y, dp], a2a_r.at[0])
    own_g.start()

    @pl.loop(1, 128)
    def _(k):
        to = (d + k) % 128
        remote(gsend.at[to], grecv.at[y, dp], a2a_s.at[0], a2a_r.at[0], (to // 4, to % 4)).start()

    await_bytes(pall.at[far, c, pl.ds(0, 128)], ag_r.at[2])
    await_bytes(pall.at[far, c, pl.ds(128, 128)], ag_r.at[3])
    mate = (dp_of(z, x, 1 - c), y)
    for n, at in enumerate((up, down, far)):
        launch(remote(pall.at[at, c], pall.at[at, c], ag_s.at[4 + n], ag_r.at[4 + n], mate))

    first_rows(4, 8)
    pre[pl.ds(0, 256), :] = dot(hid[...], wv[1])

    @pl.loop(0, 8)
    def _(i):
        start = pl.multiple_of(i * 32, 32)
        out = norm_gelu(pre, gain1, shift1, xhat1, der1, rstd1, start, 32)
        frm[pl.ds(start, 32), :] = out.astype(BF)

    place = (iota((256, 256), 0) == tgt_ref[...]).astype(F32).astype(BF)
    slots[...] = dot(place, frm[...]).astype(BF)
    for n, at in enumerate((up, down, far)):
        await_bytes(pall.at[at, 1 - c], ag_r.at[4 + n])
    for m in range(4):
        width = pall[m].reshape(512, 320)
        psend[m] = dot(slots[...], width).astype(BF).reshape(32, 8, 320)

    await_bytes(grecv, a2a_r.at[0])
    own_p = pltpu.make_async_copy(psend.at[y, dp], precv.at[d], a2a_r.at[1])
    own_p.start()

    @pl.loop(1, 128)
    def _(k):
        to = (d + k) % 128
        remote(psend.at[to % 4, to // 4], precv.at[d], a2a_s.at[1], a2a_r.at[1], (to // 4, to % 4)).start()

    total = None
    for m in range(4):
        width = pall[m].reshape(512, 320)
        part = dot(grecv[m].reshape(256, 320), width, NT)
        total = part if total is None else total + part
    grad_frames = dot(place, total.astype(BF), TN)
    gh[pl.ds(0, 256), :] = grad_frames

    sizes = dict(x=x, y=y, z=z)

    def peer(axis, k):
        if axis == "x":
            return (dp_of(z, (x + k) % 4, c), y)
        if axis == "z":
            return (dp_of((z + k) % 4, x, c), y)
        return (dp, (y + k) % 4)

    def chunk(ref, lead, dims, axis, at):
        pos = dims.index(axis)
        return ref.at[tuple(lead) + (slice(None),) * pos + (at,)]

    def scatter(source, landing, lead, dims, axis, sem):
        for k in range(1, 4):
            at = (sizes[axis] + k) % 4
            launch(
                remote(
                    chunk(source, lead, dims, axis, at),
                    landing.at[tuple(lead) + (k - 1,)],
                    rs_s.at[sem, k - 1],
                    rs_r.at[sem],
                    peer(axis, k),
                )
            )

    def gather(source, landing, lead, dims, axis, sem):
        await_bytes(landing.at[tuple(lead) + (pl.ds(0, 3),)], rs_r.at[sem])
        total = chunk(source, lead, dims, axis, sizes[axis])[...].astype(F32)
        for k in range(3):
            total = total + landing[tuple(lead) + (k,)].astype(F32)
        return total

    def norm_back(upstream, gain, xhat, der, rstd, start, rows, count, sums):
        dy = upstream * der[pl.ds(start, count), :]
        normal = xhat[pl.ds(start, count), :]
        dyn = dy * normal
        dg = sums[0] + dyn.reshape(count // 8, 8, 512).sum(axis=0)
        ds = sums[1] + dy.reshape(count // 8, 8, 512).sum(axis=0)
        mean_d = jnp.mean(dy * gain, axis=-1, keepdims=True)
        mean_dn = jnp.mean(dyn * gain, axis=-1, keepdims=True)
        inv = rstd[pl.ds(start, count), :][:, 0:1]
        return inv * (dy * gain - mean_d - normal * mean_dn), (dg, ds)

    def put_norm(layer, sums):
        for half in range(2):
            row = sums[half].sum(axis=0, keepdims=True)
            for j in range(4):
                nrm[layer * 8 + half * 4 + j : layer * 8 + half * 4 + j + 1, :] = row[:, j * LANE : (j + 1) * LANE]

    zeros = (jnp.zeros((8, 512), F32), jnp.zeros((8, 512), F32))

    def second_body(i, sums):
        start = pl.multiple_of(i * 32, 32)
        out, sums = norm_back(gh[pl.ds(start, 32), :], gain1, xhat1, der1, rstd1, start, None, 32, sums)
        gf[pl.ds(start, 32), :] = out.astype(BF)
        return sums

    sums1 = lax.fori_loop(0, 8, second_body, zeros)
    put_norm(1, sums1)
    grad_second = gf[pl.ds(0, 256), :]
    for h in range(2):
        gh[pl.ds(h * 256, 256), :] = dot(grad_second, wv[1, pl.ds(h * 512, 512), :], NT).astype(BF).astype(F32)

    for h in range(8):
        part = dot(hid[:, h * 128 : (h + 1) * 128], grad_second, TN).astype(BF)
        for j in range(4):
            convp[1, j, h // 2, (h % 2) * 2 : (h % 2) * 2 + 2] = part[:, j * LANE : (j + 1) * LANE].reshape(2, 2, 4, 8, LANE)
    for j in range(4):
        launch(remote(convp.at[1, j, :, :, 1 - c], convr.at[1, j], rs_s.at[j, 3], rs_r.at[j], mate))

    for m in range(4):
        part = dot(slots[...], grecv[m].reshape(256, 320), TN).astype(BF)
        projp[m] = part.reshape(4, 4, 2, 16, 320)
    for m in range(4):
        launch(remote(projp.at[m, :, :, 1 - c], projr.at[m], rs_s.at[4 + m, 3], rs_r.at[4 + m], mate))

    conv_orders = (("x", "y", "z"), ("y", "z", "x"), ("z", "x", "y"), ("x", "z", "y"))
    proj_orders = (("x", "z"), ("z", "x"), ("x", "z"), ("z", "x"))

    def conv_core(layer, j, sem):
        await_bytes(convr.at[layer, j], rs_r.at[sem])
        convb[layer, j] = (
            convp[layer, j, :, :, c].astype(F32) + convr[layer, j].astype(F32)
        ).astype(BF)

    def without(dims, axis):
        return tuple(one for one in dims if one != axis)

    base = ("z", "x", "y")

    def conv_send(stage, layer, j, sem):
        order = conv_orders[j]
        source, landing = ((convb, conv1), (convb1, conv2), (convb2, conv3))[stage]
        dims = base
        for one in order[:stage]:
            dims = without(dims, one)
        scatter(source, landing, (layer, j), dims, order[stage], sem)

    def conv_take(stage, layer, j, sem):
        order = conv_orders[j]
        source, landing = ((convb, conv1), (convb1, conv2), (convb2, conv3))[stage]
        dims = base
        for one in order[:stage]:
            dims = without(dims, one)
        total = gather(source, landing, (layer, j), dims, order[stage], sem)
        if stage == 0:
            convb1[layer, j] = total.astype(BF)
        elif stage == 1:
            convb2[layer, j] = total.astype(BF)
        else:
            gconv_out[layer, :, j * LANE : (j + 1) * LANE] = total

    for j in range(4):
        conv_core(1, j, j)
        conv_send(0, 1, j, 16 + j)

    def first_body(i, sums):
        start = pl.multiple_of(i * 32, 32)
        out, sums = norm_back(gh[pl.ds(start, 32), :], gain0, xhat0, der0, rstd0, start, None, 32, sums)
        gf[pl.ds(start, 32), :] = out.astype(BF)
        return sums

    sums0 = lax.fori_loop(0, 16, first_body, zeros)
    put_norm(0, sums0)

    grad_first = gf[...]
    for h in range(8):
        part = dot(act[:, h * 128 : (h + 1) * 128], grad_first, TN).astype(BF)
        for j in range(4):
            convp[0, j, h // 2, (h % 2) * 2 : (h % 2) * 2 + 2] = part[:, j * LANE : (j + 1) * LANE].reshape(2, 2, 4, 8, LANE)
    for j in range(4):
        launch(remote(convp.at[0, j, :, :, 1 - c], convr.at[0, j], rs_s.at[8 + j, 3], rs_r.at[8 + j], mate))
    to_mate = remote(nrm, nrmr, nm_s.at[0, 0], nm_r.at[0], mate)
    to_mate.start()

    for m in range(4):
        await_bytes(projr.at[m], rs_r.at[4 + m])
        projb[m] = (projp[m, :, :, c].astype(F32) + projr[m].astype(F32)).astype(BF)
        scatter(projb, proj1, (m,), ("z", "x"), proj_orders[m][0], 12 + m)
    for j in range(4):
        conv_core(0, j, 8 + j)
        conv_send(0, 0, j, 20 + j)
    for j in range(4):
        conv_take(0, 1, j, 16 + j)
        conv_send(1, 1, j, 24 + j)
    for m in range(4):
        projb1[m] = gather(projb, proj1, (m,), ("z", "x"), proj_orders[m][0], 12 + m).astype(BF)
        scatter(projb1, proj2, (m,), (proj_orders[m][1],), proj_orders[m][1], 36 + m)

    for h in range(2):
        gx[pl.ds(h * 256, 256), :] = dot(gf[pl.ds(h * 256, 256), :], wv[0], NT)

    @pl.loop(0, 8)
    def _(i):
        for h in range(2):
            rows = gx[pl.ds(pl.multiple_of(h * 256 + i * 32, 32), 32), :]
            for k in range(2):
                for j in range(4):
                    xo[j, pl.ds(2 * h + k, 32, stride=4), :] = rows[:, k * 512 + j * LANE : k * 512 + (j + 1) * LANE]
        out = jnp.concatenate([xo[j] for j in range(4)], axis=1)
        gfv[pl.ds(pl.multiple_of(i * 128, 128), 128), :] = out.astype(BF)

    feat_out = pltpu.make_async_copy(gfv, gfeat_out, out_sem.at[0])
    feat_out.start()

    turn = ((iota((128, 1024), 1) >> 3) == iota((128, 1024), 0)).astype(F32).astype(BF)
    pick_t = (iota((512, 128), 1) == dp).astype(F32).astype(BF)
    wanted_t = dot(dot(pick_t, table, NT).astype(BF), turn)
    r_id = (iota((512, 1024), 1) & 7).astype(F32)
    c_id = iota((512, 1024), 0).astype(F32)
    query[...] = (wanted_t * 8.0 + r_id == c_id).astype(F32).astype(BF)
    await_bytes(precv, a2a_r.at[1])
    packv[...] = dot(query[...], precv[...].reshape(1024, 320)).astype(BF)
    pack_out = pltpu.make_async_copy(packv, packed_out, out_sem.at[1])
    pack_out.start()

    def norm_stage(stage, axis):
        copies = []
        for k in range(1, 4):
            copies.append(
                remote(nrm, nrm1.at[stage, k - 1], nm_s.at[1 + stage, k - 1], nm_r.at[1 + stage], peer(axis, k))
            )
            copies[-1].start()
        return copies

    def norm_take(stage, copies):
        await_bytes(nrm1.at[stage], nm_r.at[1 + stage])
        for one in copies:
            one.wait_send()
        nrm[...] = nrm[...] + nrm1[stage, 0] + nrm1[stage, 1] + nrm1[stage, 2]

    await_bytes(nrmr, nm_r.at[0])
    to_mate.wait_send()
    nrm[...] = nrm[...] + nrmr[...]
    moving = norm_stage(0, "x")
    norm_take(0, moving)
    for j in range(4):
        conv_take(0, 0, j, 20 + j)
        conv_send(1, 0, j, 28 + j)
    moving = norm_stage(1, "y")
    norm_take(1, moving)
    for j in range(4):
        conv_take(1, 1, j, 24 + j)
        conv_send(2, 1, j, 32 + j)
    for m in range(4):
        projb2[m] = gather(projb1, proj2, (m,), (proj_orders[m][1],), proj_orders[m][1], 36 + m).astype(BF)
    scatter(projb2, proj3, (), ("y",), "y", 40)
    for j in range(4):
        conv_take(1, 0, j, 28 + j)
        conv_send(2, 0, j, 44 + j)
    moving = norm_stage(2, "z")
    norm_take(2, moving)
    gnorm_out[...] = nrm[...]
    for j in range(4):
        conv_take(2, 1, j, 32 + j)
    gproj_out[...] = gather(projb2, proj3, (), ("y",), "y", 40)
    for j in range(4):
        conv_take(2, 0, j, 44 + j)

    for one in sends:
        one.wait_send()
    await_bytes(gsend.at[pl.ds(0, 127)], a2a_s.at[0])
    await_bytes(precv.at[pl.ds(0, 127)], a2a_s.at[1])
    feat_out.wait()
    pack_out.wait()


def local(features, lengths, dests, offsets, conv_weight, norm_gain, norm_shift, proj_weight, grad_packed):
    steps = jnp.arange(8, dtype=jnp.int32)[None, :]
    rows = dests[:, None] * 8 + (offsets & 7)[:, None] + steps
    target = jnp.where(steps < lengths[:, None], rows, -1).reshape(1, 256)
    pair_dest, pair_block = dests[0::2], offsets[0::2] >> 3
    named = pair_dest[:, None] == jnp.arange(LANE, dtype=jnp.int32)[None, :]
    index_row = jnp.min(jnp.where(named, pair_block[:, None], 64), axis=0, keepdims=True).astype(F32)
    vmem = pl.BlockSpec(memory_space=pltpu.VMEM)
    hbm = pl.BlockSpec(memory_space=pl.ANY)
    V = pltpu.VMEM
    D = pltpu.SemaphoreType.DMA
    scratch = [
        V((1024, 512), BF), V((2, 1024, 512), BF), V((512, 320), BF), V((4, 128, LANE), F32),
        V((512, 1024), BF), V((512, 512), F32), V((512, 512), F32), V((512, 512), F32), V((512, LANE), F32),
        V((256, 512), F32), V((256, 512), F32), V((256, LANE), F32),
        V((256, 1024), BF), V((256, 512), BF), V((256, 512), BF),
        V((4, 8, 4, 1, LANE), F32), V((512, 1024), BF), V((128, 8, 320), BF), V((4, 32, 8, 320), BF),
        V((4, 32, 8, 320), BF), V((128, 8, 320), BF), V((4, 2, 256, 320), BF), V((512, 320), BF),
        V((512, 512), F32), V((512, 512), BF), V((512, 1024), F32), V((4, 128, LANE), F32), V((1024, 512), BF),
        V((2, 4, 4, 4, 2, 4, 8, LANE), BF), V((2, 4, 4, 4, 4, 8, LANE), BF), V((2, 4, 4, 4, 4, 8, LANE), BF),
        V((2, 4, 3, 4, 4, 8, LANE), BF), V((2, 4, 4, 4, 8, LANE), BF),
        V((2, 4, 3, 4, 8, LANE), BF), V((2, 4, 4, 8, LANE), BF), V((2, 4, 3, 8, LANE), BF),
        V((4, 4, 4, 2, 16, 320), BF), V((4, 4, 4, 16, 320), BF), V((4, 4, 4, 16, 320), BF),
        V((4, 3, 4, 16, 320), BF), V((4, 4, 16, 320), BF), V((4, 3, 16, 320), BF), V((4, 16, 320), BF), V((3, 16, 320), BF),
        V((16, LANE), F32), V((16, LANE), F32), V((3, 3, 16, LANE), F32),
        D((4,)), D((2,)), D((13,)), D((3,)), D((7,)), D((7,)), D((2,)), D((2,)), D((48, 4)), D((48,)), D((4, 3)), D((4,)),
    ]
    packed, gfeat, gconv, gproj, gnorm = pl.pallas_call(
        kernel,
        out_shape=(
            jax.ShapeDtypeStruct((512, 320), BF),
            jax.ShapeDtypeStruct((1024, 512), BF),
            jax.ShapeDtypeStruct((2, 8, 512), F32),
            jax.ShapeDtypeStruct((16, 320), F32),
            jax.ShapeDtypeStruct((16, LANE), F32),
        ),
        in_specs=[vmem] * 4 + [hbm] * 4,
        out_specs=(hbm, hbm, vmem, vmem, vmem),
        scratch_shapes=scratch,
        compiler_params=pltpu.CompilerParams(collective_id=0, has_side_effects=True),
    )(
        index_row, target, norm_gain, norm_shift, features.reshape(1024, 512), conv_weight,
        proj_weight.reshape(2, 256, 320), grad_packed,
    )
    at = (lax.axis_index("dp") * 4 + lax.axis_index("mp")) * 8
    grad_norm = lax.dynamic_slice(gnorm.reshape(2, 1024), (0, at), (2, 8))
    return packed, gfeat.reshape(32, 32, 512), gconv, grad_norm, gproj


def solution(mesh):
    return jax.shard_map(
        local,
        mesh=mesh,
        in_specs=(
            P(("dp", "mp"), None, None),
            P(("dp", "mp")),
            P(("dp", "mp")),
            P(("dp", "mp")),
            P(),
            P(),
            P(),
            P(None, "mp"),
            P("dp", "mp"),
        ),
        out_specs=(
            P("dp", "mp"),
            P(("dp", "mp"), None, None),
            P(None, ("dp", "mp"), None),
            P(None, ("dp", "mp")),
            P("dp", "mp"),
        ),
        check_vma=False,
    )
```

```python
import jax
import jax.numpy as jnp
from jax import lax
from jax.experimental import pallas as pl
from jax.experimental.pallas import tpu as pltpu
from jax.sharding import PartitionSpec as P

EPSILON = 1e-05
BF = jnp.bfloat16
F32 = jnp.float32
MESH = pl.DeviceIdType.MESH
NN = (((1,), (0,)), ((), ()))
NT = (((1,), (1,)), ((), ()))
TN = (((0,), (0,)), ((), ()))
LANE = 128


def dot(a, b, dims=NN):
    return lax.dot_general(a, b, dims, preferred_element_type=F32)


def iota(shape, dim):
    return lax.broadcasted_iota(jnp.int32, shape, dim)


def kernel(
    len_ref, dest_ref, off_ref, gain_ref, shift_ref, feat_hbm, weight_hbm, proj_hbm, gp_hbm,
    packed_out, gfeat_out, gconv_out, gproj_out, gnorm_out,
    xb, wv, gpv, xf, act, pre, xhat0, der0, rstd0, xhat1, der1, rstd1, hid, frm, slots,
    tbl, query, gsend, grecv, psend, precv, pall,
    gh, gf, gx, xo,
    convp, convr, convb, conv1, convb1, conv2, convb2, conv3,
    projp, projr, projb, proj1, projb1, proj2, projb2, proj3,
    nrm, nrmr, nrm1,
    in_sem, idx_s, idx_r, ag_s, ag_r, a2a_s, a2a_r, rs_s, rs_r, nm_s, nm_r,
):
    dp = lax.axis_index("dp")
    y = lax.axis_index("mp")
    z, q = dp // 8, dp % 8
    x, c = q // 2, q % 2
    d = dp * 4 + y

    def dp_of(zz, xx, cc):
        return zz * 8 + xx * 2 + cc

    def remote(src, dst, ssem, rsem, to):
        return pltpu.make_async_remote_copy(
            src_ref=src, dst_ref=dst, send_sem=ssem, recv_sem=rsem, device_id=to, device_id_type=MESH
        )

    def await_bytes(ref, sem):
        pltpu.make_async_copy(ref, ref, sem).wait()

    loads = [
        pltpu.make_async_copy(feat_hbm, xb, in_sem.at[0]),
        pltpu.make_async_copy(weight_hbm, wv, in_sem.at[1]),
        pltpu.make_async_copy(proj_hbm, pall.at[y], in_sem.at[2]),
        pltpu.make_async_copy(gp_hbm, gpv, in_sem.at[3]),
    ]
    for one in (2, 0, 1, 3):
        loads[one].start()

    partners = (
        [(dp, (y + k) % 4) for k in range(1, 4)]
        + [(z * 8 + (q + k) % 8, y) for k in range(1, 8)]
        + [(((z + k) % 4) * 8 + q, y) for k in range(1, 4)]
    )
    barrier = pltpu.get_barrier_semaphore()
    for to in partners:
        pl.semaphore_signal(barrier, inc=1, device_id=to, device_id_type=MESH)

    lane = iota((1, LANE), 1)
    row = jnp.full((1, LANE), 64, jnp.int32)
    for p in range(16):
        row = jnp.where(lane == dest_ref[2 * p], off_ref[2 * p] >> 3, row)
    tbl[z, q, y] = row.astype(F32)
    lane = iota((1, 256), 1)
    utterance, step = lane >> 3, lane & 7
    target = jnp.full((1, 256), -1, jnp.int32)
    for u in range(32):
        at = jnp.where(step < len_ref[u], dest_ref[u] * 8 + (off_ref[u] & 7) + step, -1)
        target = jnp.where(utterance == u, at, target)
    place = (iota((256, 256), 0) == target).astype(F32).astype(BF)

    loads[0].wait()

    @pl.loop(0, 8)
    def _(i):
        rows = xb[pl.ds(pl.multiple_of(i * 128, 128), 128), :].astype(F32)
        for j in range(4):
            xf[j] = rows[:, j * LANE : (j + 1) * LANE]
        for k in range(4):
            part = jnp.concatenate([xf[j, pl.ds(k, 32, stride=4), :] for j in range(4)], axis=1)
            act[pl.ds(pl.multiple_of((k // 2) * 256 + i * 32, 32), 32), (k % 2) * 512 : (k % 2) * 512 + 512] = part.astype(BF)

    pl.semaphore_wait(barrier, len(partners))

    sends = []

    def launch(copy):
        copy.start()
        sends.append(copy)

    for k in range(1, 4):
        launch(remote(tbl.at[z, q, y], tbl.at[z, q, y], idx_s.at[k - 1], idx_r.at[0], (dp, (y + k) % 4)))
    loads[2].wait()
    up, down, far = (y + 1) % 4, (y + 3) % 4, (y + 2) % 4
    launch(remote(pall.at[y, c], pall.at[y, c], ag_s.at[0], ag_r.at[0], (dp, up)))
    launch(remote(pall.at[y, c], pall.at[y, c], ag_s.at[1], ag_r.at[1], (dp, down)))

    loads[1].wait()
    pre[...] = dot(act[...], wv[0])

    await_bytes(tbl.at[z, q, pl.ds(0, 3)], idx_r.at[0])
    for k in range(1, 8):
        launch(remote(tbl.at[z, q], tbl.at[z, q], idx_s.at[2 + k], idx_r.at[1], (z * 8 + (q + k) % 8, y)))

    def norm_gelu(source, gain, shift, xhat, der, rstd, start, count):
        v = source[pl.ds(start, count), :]
        mean = jnp.mean(v, axis=-1, keepdims=True)
        centred = v - mean
        spread = jnp.mean(centred * centred, axis=-1, keepdims=True)
        inv = lax.rsqrt(spread + EPSILON)
        normal = centred * inv
        arg = normal * gain + shift
        cdf = 0.5 + 0.5 * lax.erf(arg * (2.0**-0.5))
        xhat[pl.ds(start, count), :] = normal
        der[pl.ds(start, count), :] = cdf + arg * (jnp.exp(-0.5 * arg * arg) * 0.3989422804014327)
        rstd[pl.ds(start, count), :] = jnp.broadcast_to(inv, (count, LANE))
        return arg * cdf

    gain0, shift0 = gain_ref[0:1, :], shift_ref[0:1, :]
    gain1, shift1 = gain_ref[1:2, :], shift_ref[1:2, :]

    def first_rows(lo, hi):
        @pl.loop(lo, hi)
        def _(i):
            start = pl.multiple_of(i * 32, 32)
            for h in range(2):
                out = norm_gelu(pre, gain0, shift0, xhat0, der0, rstd0, pl.multiple_of(start + h * 256, 32), 32)
                hid[pl.ds(start, 32), h * 512 : (h + 1) * 512] = out.astype(BF)

    first_rows(0, 4)

    await_bytes(tbl.at[z, pl.ds(0, 7)], idx_r.at[1])
    for k in range(1, 4):
        launch(remote(tbl.at[z], tbl.at[z], idx_s.at[9 + k], idx_r.at[2], (((z + k) % 4) * 8 + q, y)))

    first_rows(4, 8)
    await_bytes(pall.at[down, c], ag_r.at[0])
    launch(remote(pall.at[down, c, pl.ds(0, 80)], pall.at[down, c, pl.ds(0, 80)], ag_s.at[2], ag_r.at[2], (dp, up)))
    await_bytes(pall.at[up, c], ag_r.at[1])
    launch(remote(pall.at[up, c, pl.ds(80, 80)], pall.at[up, c, pl.ds(80, 80)], ag_s.at[3], ag_r.at[3], (dp, down)))

    loads[3].wait()
    await_bytes(tbl.at[pl.ds(0, 3)], idx_r.at[2])
    table = tbl[...].reshape(128, LANE).astype(BF)
    pick = (iota((128, 512), 0) == dp).astype(F32).astype(BF)
    blocks = dot(table, pick).astype(BF)
    row_id = iota((256, 512), 0)
    column = (iota((256, 512), 1) - (row_id & 7)).astype(F32)

    own_g = pltpu.make_async_copy(gsend.at[d], grecv.at[y, dp], a2a_r.at[0])
    for turn in range(4):
        part = (z + turn) % 4
        spread = ((iota((256, 128), 0) >> 3) + part * 32 == iota((256, 128), 1)).astype(F32).astype(BF)
        one_hot = (dot(spread, blocks) * 8.0 == column).astype(F32).astype(BF)
        query[pl.ds(pl.multiple_of(part * 256, 256), 256), :] = one_hot
        gsend[pl.ds(part * 32, 32)] = dot(one_hot, gpv[...], NT).astype(BF).reshape(32, 8, 320)
        if turn == 0:
            own_g.start()

        @pl.loop(0, 8)
        def _(k):
            to = part * 8 + (q + k) % 8
            for m in range(4):
                if turn == 0 and m == 0:

                    @pl.when(k > 0)
                    def _():
                        remote(gsend.at[to * 4 + y], grecv.at[y, dp], a2a_s.at[0], a2a_r.at[0], (to, y)).start()
                else:
                    side = (y + m) % 4
                    remote(gsend.at[to * 4 + side], grecv.at[y, dp], a2a_s.at[0], a2a_r.at[0], (to, side)).start()

    await_bytes(pall.at[far, c, pl.ds(0, 80)], ag_r.at[2])
    await_bytes(pall.at[far, c, pl.ds(80, 80)], ag_r.at[3])
    mate = (dp_of(z, x, 1 - c), y)
    for n, at in enumerate((up, down, far)):
        launch(remote(pall.at[at, c], pall.at[at, c], ag_s.at[4 + n], ag_r.at[4 + n], mate))

    pre[pl.ds(0, 256), :] = dot(hid[...], wv[1])

    @pl.loop(0, 4)
    def _(i):
        for h in range(2):
            start = pl.multiple_of(i * 64 + h * 32, 32)
            out = norm_gelu(pre, gain1, shift1, xhat1, der1, rstd1, start, 32)
            frm[pl.ds(start, 32), :] = out.astype(BF)

    slots[...] = dot(place, frm[...]).astype(BF)
    for n, at in enumerate((up, down, far)):
        await_bytes(pall.at[at, 1 - c], ag_r.at[4 + n])
    for m in range(4):
        psend[m] = dot(slots[...], pall[m].reshape(320, 512), NT).astype(BF).reshape(32, 8, 320)

    own_p = pltpu.make_async_copy(psend.at[y, dp], precv.at[d], a2a_r.at[1])
    own_p.start()

    @pl.loop(0, 32)
    def _(k):
        to = (dp + k) % 32
        for m in range(4):
            side = (y + m) % 4
            copy = remote(psend.at[side, to], precv.at[d], a2a_s.at[1], a2a_r.at[1], (to, side))
            if m == 0:
                pl.when(k > 0)(copy.start)
            else:
                copy.start()

    await_bytes(grecv, a2a_r.at[0])

    total = None
    for m in range(4):
        part = dot(grecv[m].reshape(256, 320), pall[m].reshape(320, 512))
        total = part if total is None else total + part
    grad_frames = dot(place, total.astype(BF), TN)
    gh[pl.ds(0, 256), :] = grad_frames

    sizes = dict(x=x, y=y, z=z)

    def peer(axis, k):
        if axis == "x":
            return (dp_of(z, (x + k) % 4, c), y)
        if axis == "z":
            return (dp_of((z + k) % 4, x, c), y)
        return (dp, (y + k) % 4)

    def chunk(ref, lead, dims, axis, at):
        pos = dims.index(axis)
        return ref.at[tuple(lead) + (slice(None),) * pos + (at,)]

    def scatter(source, landing, lead, dims, axis, sem):
        for k in range(1, 4):
            at = (sizes[axis] + k) % 4
            launch(
                remote(
                    chunk(source, lead, dims, axis, at),
                    landing.at[tuple(lead) + (k - 1,)],
                    rs_s.at[sem, k - 1],
                    rs_r.at[sem],
                    peer(axis, k),
                )
            )

    def gather(source, landing, lead, dims, axis, sem):
        await_bytes(landing.at[tuple(lead) + (pl.ds(0, 3),)], rs_r.at[sem])
        total = chunk(source, lead, dims, axis, sizes[axis])[...].astype(F32)
        for k in range(3):
            total = total + landing[tuple(lead) + (k,)].astype(F32)
        return total

    def norm_back(upstream, gain, xhat, der, rstd, start, count, sums):
        dy = upstream * der[pl.ds(start, count), :]
        normal = xhat[pl.ds(start, count), :]
        dyn = dy * normal
        dg = sums[0] + dyn.reshape(count // 8, 8, 512).sum(axis=0)
        ds = sums[1] + dy.reshape(count // 8, 8, 512).sum(axis=0)
        mean_d = jnp.mean(dy * gain, axis=-1, keepdims=True)
        mean_dn = jnp.mean(dyn * gain, axis=-1, keepdims=True)
        inv = rstd[pl.ds(start, count), :][:, 0:1]
        return inv * (dy * gain - mean_d - normal * mean_dn), (dg, ds)

    def put_norm(layer, sums):
        for half in range(2):
            row = sums[half].sum(axis=0, keepdims=True)
            for j in range(4):
                nrm[layer * 8 + half * 4 + j : layer * 8 + half * 4 + j + 1, :] = row[:, j * LANE : (j + 1) * LANE]

    zeros = (jnp.zeros((8, 512), F32), jnp.zeros((8, 512), F32))

    def second_body(i, sums):
        for h in range(2):
            start = pl.multiple_of(i * 64 + h * 32, 32)
            out, sums = norm_back(gh[pl.ds(start, 32), :], gain1, xhat1, der1, rstd1, start, 32, sums)
            gf[pl.ds(start, 32), :] = out.astype(BF)
        return sums

    sums1 = lax.fori_loop(0, 4, second_body, zeros)
    put_norm(1, sums1)
    grad_second = gf[pl.ds(0, 256), :]
    for h in range(2):
        gh[pl.ds(h * 256, 256), :] = dot(grad_second, wv[1, pl.ds(h * 512, 512), :], NT).astype(BF).astype(F32)

    for h in range(8):
        part = dot(hid[:, h * 128 : (h + 1) * 128], grad_second, TN).astype(BF)
        for j in range(4):
            convp[1, j, h // 2, (h % 2) * 2 : (h % 2) * 2 + 2] = part[:, j * LANE : (j + 1) * LANE].reshape(2, 2, 4, 8, LANE)
    for j in range(4):
        launch(remote(convp.at[1, j, :, :, 1 - c], convr.at[1, j], rs_s.at[j, 3], rs_r.at[j], mate))

    for m in range(4):
        part = dot(slots[...], grecv[m].reshape(256, 320), TN).astype(BF)
        projp[m] = part.reshape(4, 4, 2, 16, 320)
    for m in range(4):
        launch(remote(projp.at[m, :, :, 1 - c], projr.at[m], rs_s.at[4 + m, 3], rs_r.at[4 + m], mate))

    conv_orders = (
        (("x", "y", "z"), ("y", "z", "x"), ("z", "x", "y"), ("x", "z", "y")),
        (("y", "x", "z"), ("y", "z", "x"), ("y", "x", "z"), ("y", "z", "x")),
    )
    proj_orders = (("x", "z"), ("z", "x"), ("x", "z"), ("z", "x"))

    def conv_core(layer, j, sem):
        await_bytes(convr.at[layer, j], rs_r.at[sem])
        convb[layer, j] = (
            convp[layer, j, :, :, c].astype(F32) + convr[layer, j].astype(F32)
        ).astype(BF)

    def without(dims, axis):
        return tuple(one for one in dims if one != axis)

    base = ("z", "x", "y")

    def conv_send(stage, layer, j, sem):
        order = conv_orders[layer][j]
        source, landing = ((convb, conv1), (convb1, conv2), (convb2, conv3))[stage]
        dims = base
        for one in order[:stage]:
            dims = without(dims, one)
        scatter(source, landing, (layer, j), dims, order[stage], sem)

    def conv_take(stage, layer, j, sem):
        order = conv_orders[layer][j]
        source, landing = ((convb, conv1), (convb1, conv2), (convb2, conv3))[stage]
        dims = base
        for one in order[:stage]:
            dims = without(dims, one)
        total = gather(source, landing, (layer, j), dims, order[stage], sem)
        if stage == 0:
            convb1[layer, j] = total.astype(BF)
        elif stage == 1:
            convb2[layer, j] = total.astype(BF)
        else:
            gconv_out[layer, :, j * LANE : (j + 1) * LANE] = total

    for j in range(4):
        conv_core(1, j, j)
        conv_send(0, 1, j, 16 + j)

    def first_body(i, sums):
        for h in range(2):
            start = pl.multiple_of(i * 64 + h * 32, 32)
            out, sums = norm_back(gh[pl.ds(start, 32), :], gain0, xhat0, der0, rstd0, start, 32, sums)
            gf[pl.ds(start, 32), :] = out.astype(BF)
        return sums

    sums0 = lax.fori_loop(0, 8, first_body, zeros)
    put_norm(0, sums0)
    to_mate = remote(nrm, nrmr, nm_s.at[0, 0], nm_r.at[0], mate)
    to_mate.start()

    grad_first = gf[...]
    for h in range(8):
        part = dot(act[:, h * 128 : (h + 1) * 128], grad_first, TN).astype(BF)
        for j in range(4):
            convp[0, j, h // 2, (h % 2) * 2 : (h % 2) * 2 + 2] = part[:, j * LANE : (j + 1) * LANE].reshape(2, 2, 4, 8, LANE)
    for j in range(4):
        launch(remote(convp.at[0, j, :, :, 1 - c], convr.at[0, j], rs_s.at[8 + j, 3], rs_r.at[8 + j], mate))

    def norm_stage(stage, axis):
        copies = []
        for k in range(1, 4):
            copies.append(
                remote(nrm, nrm1.at[stage, k - 1], nm_s.at[1 + stage, k - 1], nm_r.at[1 + stage], peer(axis, k))
            )
            copies[-1].start()
        return copies

    def norm_take(stage, copies):
        await_bytes(nrm1.at[stage], nm_r.at[1 + stage])
        for one in copies:
            one.wait_send()
        nrm[...] = nrm[...] + nrm1[stage, 0] + nrm1[stage, 1] + nrm1[stage, 2]

    await_bytes(nrmr, nm_r.at[0])
    to_mate.wait_send()
    nrm[...] = nrm[...] + nrmr[...]
    moving = norm_stage(0, "x")

    for m in range(4):
        await_bytes(projr.at[m], rs_r.at[4 + m])
        projb[m] = (projp[m, :, :, c].astype(F32) + projr[m].astype(F32)).astype(BF)
        scatter(projb, proj1, (m,), ("z", "x"), proj_orders[m][0], 12 + m)
    for j in range(4):
        conv_core(0, j, 8 + j)
        conv_send(0, 0, j, 20 + j)

    for h in range(2):
        gx[pl.ds(h * 256, 256), :] = dot(gf[pl.ds(h * 256, 256), :], wv[0], NT)

    norm_take(0, moving)
    moving = norm_stage(1, "y")

    for j in range(4):
        conv_take(0, 1, j, 16 + j)
        conv_send(1, 1, j, 24 + j)

    @pl.loop(0, 8)
    def _(i):
        for h in range(2):
            rows = gx[pl.ds(pl.multiple_of(h * 256 + i * 32, 32), 32), :]
            for k in range(2):
                for j in range(4):
                    xo[j, pl.ds(2 * h + k, 32, stride=4), :] = rows[:, k * 512 + j * LANE : k * 512 + (j + 1) * LANE]
        out = jnp.concatenate([xo[j] for j in range(4)], axis=1)
        gfeat_out[pl.ds(pl.multiple_of(i * 128, 128), 128), :] = out.astype(BF)

    for m in range(4):
        projb1[m] = gather(projb, proj1, (m,), ("z", "x"), proj_orders[m][0], 12 + m).astype(BF)
        scatter(projb1, proj2, (m,), (proj_orders[m][1],), proj_orders[m][1], 36 + m)

    norm_take(1, moving)
    moving = norm_stage(2, "z")
    for j in range(4):
        conv_take(0, 0, j, 20 + j)
        conv_send(1, 0, j, 28 + j)

    await_bytes(precv, a2a_r.at[1])
    packed_out[...] = dot(precv[...].reshape(1024, 320), query[...], TN).astype(BF)

    for j in range(4):
        conv_take(1, 1, j, 24 + j)
        conv_send(2, 1, j, 32 + j)
    for m in range(4):
        projb2[m] = gather(projb1, proj2, (m,), (proj_orders[m][1],), proj_orders[m][1], 36 + m).astype(BF)
    scatter(projb2, proj3, (), ("y",), "y", 40)
    for j in range(4):
        conv_take(1, 0, j, 28 + j)
        conv_send(2, 0, j, 44 + j)
    norm_take(2, moving)
    gnorm_out[...] = nrm[...]
    for j in range(4):
        conv_take(2, 1, j, 32 + j)
    gproj_out[...] = gather(projb2, proj3, (), ("y",), "y", 40)
    for j in range(4):
        conv_take(2, 0, j, 44 + j)

    for one in sends:
        one.wait_send()
    await_bytes(gsend.at[pl.ds(0, 127)], a2a_s.at[0])
    await_bytes(precv.at[pl.ds(0, 127)], a2a_s.at[1])


def finish(
    packed_in, gfeat_in, gconv_in, gproj_in, gnorm_in, packed_out, gfeat_out, gconv_out, gproj_out, gnorm_out, sem
):
    copies = [
        pltpu.make_async_copy(packed_in, packed_out, sem.at[0]),
        pltpu.make_async_copy(gfeat_in, gfeat_out, sem.at[1]),
        pltpu.make_async_copy(gconv_in, gconv_out, sem.at[2]),
        pltpu.make_async_copy(gproj_in, gproj_out, sem.at[3]),
    ]
    for one in (1, 0, 2, 3):
        copies[one].start()
    d = lax.axis_index("dp") * 4 + lax.axis_index("mp")
    for layer in range(2):
        row = gnorm_in[pl.ds(layer * 8 + d // 16, 1), :]
        turned = pltpu.roll(row, LANE - (d % 16) * 8, 1)
        gnorm_out[layer : layer + 1, :] = turned[:, 0:8]
    for one in copies:
        one.wait()


def local(features, lengths, dests, offsets, conv_weight, norm_gain, norm_shift, proj_weight, grad_packed):
    vmem = pl.BlockSpec(memory_space=pltpu.VMEM)
    hbm = pl.BlockSpec(memory_space=pltpu.HBM)
    smem = pl.BlockSpec(memory_space=pltpu.SMEM)
    V = pltpu.VMEM
    D = pltpu.SemaphoreType.DMA
    scratch = [
        V((1024, 512), BF), V((2, 1024, 512), BF), V((320, 512), BF), V((4, 128, LANE), F32),
        V((512, 1024), BF), V((512, 512), F32), V((512, 512), F32), V((512, 512), F32), V((512, LANE), F32),
        V((256, 512), F32), V((256, 512), F32), V((256, LANE), F32),
        V((256, 1024), BF), V((256, 512), BF), V((256, 512), BF),
        V((4, 8, 4, 1, LANE), F32), V((1024, 512), BF), V((128, 8, 320), BF), V((4, 32, 8, 320), BF),
        V((4, 32, 8, 320), BF), V((128, 8, 320), BF), V((4, 2, 160, 512), BF),
        V((512, 512), F32), V((512, 512), BF), V((512, 1024), F32), V((4, 128, LANE), F32),
        V((2, 4, 4, 4, 2, 4, 8, LANE), BF), V((2, 4, 4, 4, 4, 8, LANE), BF), V((2, 4, 4, 4, 4, 8, LANE), BF),
        V((2, 4, 3, 4, 4, 8, LANE), BF), V((2, 4, 4, 4, 8, LANE), BF),
        V((2, 4, 3, 4, 8, LANE), BF), V((2, 4, 4, 8, LANE), BF), V((2, 4, 3, 8, LANE), BF),
        V((4, 4, 4, 2, 16, 320), BF), V((4, 4, 4, 16, 320), BF), V((4, 4, 4, 16, 320), BF),
        V((4, 3, 4, 16, 320), BF), V((4, 4, 16, 320), BF), V((4, 3, 16, 320), BF), V((4, 16, 320), BF), V((3, 16, 320), BF),
        V((16, LANE), F32), V((16, LANE), F32), V((3, 3, 16, LANE), F32),
        D((4,)), D((13,)), D((3,)), D((7,)), D((7,)), D((2,)), D((2,)), D((48, 4)), D((48,)), D((4, 3)), D((4,)),
    ]
    results = ((320, 512), BF), ((1024, 512), BF), ((2, 8, 512), F32), ((16, 320), F32), ((16, LANE), F32)
    middle = pl.pallas_call(
        kernel,
        out_shape=tuple(pltpu.VMEM(*one) for one in results),
        in_specs=[smem] * 3 + [vmem] * 2 + [hbm] * 4,
        out_specs=(vmem,) * 5,
        scratch_shapes=scratch,
        compiler_params=pltpu.CompilerParams(collective_id=0, has_side_effects=True, vmem_limit_bytes=65_400_000),
    )(
        lengths, dests, offsets, norm_gain, norm_shift, features.reshape(1024, 512), conv_weight,
        proj_weight.T.reshape(2, 160, 512), grad_packed.T,
    )
    shapes = (*results[:4], ((2, 8), F32))
    packed, gfeat, gconv, gproj, gnorm = pl.pallas_call(
        finish,
        out_shape=tuple(jax.ShapeDtypeStruct(*one) for one in shapes),
        in_specs=[vmem] * 5,
        out_specs=(hbm, hbm, hbm, hbm, vmem),
        scratch_shapes=[D((4,))],
    )(*[pltpu.with_memory_space_constraint(one, pltpu.VMEM) for one in middle])
    return packed.T, gfeat.reshape(32, 32, 512), gconv, gnorm, gproj


def solution(mesh):
    return jax.shard_map(
        local,
        mesh=mesh,
        in_specs=(
            P(("dp", "mp"), None, None),
            P(("dp", "mp")),
            P(("dp", "mp")),
            P(("dp", "mp")),
            P(),
            P(),
            P(),
            P(None, "mp"),
            P("dp", "mp"),
        ),
        out_specs=(
            P("dp", "mp"),
            P(("dp", "mp"), None, None),
            P(None, ("dp", "mp"), None),
            P(None, ("dp", "mp")),
            P("dp", "mp"),
        ),
        check_vma=False,
    )
```

```python
import jax
import jax.numpy as jnp
from jax import lax
from jax.experimental import pallas as pl
from jax.experimental.pallas import tpu as pltpu
from jax.sharding import PartitionSpec as P

EPSILON = 1e-05
BF = jnp.bfloat16
F32 = jnp.float32
MESH = pl.DeviceIdType.MESH
NN = (((1,), (0,)), ((), ()))
NT = (((1,), (1,)), ((), ()))
TN = (((0,), (0,)), ((), ()))
LANE = 128
WIDE = 384


def dot(a, b, dims=NN):
    return lax.dot_general(a, b, dims, preferred_element_type=F32)


def iota(shape, dim):
    return lax.broadcasted_iota(jnp.int32, shape, dim)


def kernel(
    len_ref, dest_ref, off_ref, gain_ref, shift_ref, feat_hbm, weight_hbm, proj_hbm, gp_hbm,
    packed_out, gfeat_out, gconv_out, gproj_out, gnorm_out,
    xb, wv, gpv, xf, act, actt, pre, xhat0, der0, rstd0, xhat1, der1, rstd1, hid, hidt, frm,
    tbl, query, gsend, grecv, fsend, frecv, pall, packin,
    gh, gf, gx, xo,
    convp, convr, convb, conv1, convb1, conv2,
    projp, projr, projb, proj1,
    nrm, nrmr, nrm1, nrm2,
    in_sem, idx_s, idx_r, ag_s, ag_r, a2a_s, a2a_r, fg_s, fg_r, rs_s, rs_r, nm_s, nm_r, pl_s, pl_r,
):
    dp = lax.axis_index("dp")
    y = lax.axis_index("mp")
    z, q = dp // 8, dp % 8
    x, c = q // 2, q % 2
    d = dp * 4 + y

    def dp_of(zz, xx, cc):
        return zz * 8 + xx * 2 + cc

    def remote(src, dst, ssem, rsem, to):
        return pltpu.make_async_remote_copy(
            src_ref=src, dst_ref=dst, send_sem=ssem, recv_sem=rsem, device_id=to, device_id_type=MESH
        )

    def await_bytes(ref, sem):
        pltpu.make_async_copy(ref, ref, sem).wait()

    loads = [
        pltpu.make_async_copy(feat_hbm, xb, in_sem.at[0]),
        pltpu.make_async_copy(weight_hbm, wv, in_sem.at[1]),
        pltpu.make_async_copy(proj_hbm, pall.at[y, pl.ds(0, 320)], in_sem.at[2]),
        pltpu.make_async_copy(gp_hbm, gpv.at[pl.ds(0, 320)], in_sem.at[3]),
    ]
    for one in (2, 0, 1, 3):
        loads[one].start()

    partners = (
        [(dp, (y + k) % 4) for k in range(1, 4)]
        + [(z * 8 + (q + k) % 8, y) for k in range(1, 8)]
        + [(((z + k) % 4) * 8 + q, y) for k in range(1, 4)]
    )
    barrier = pltpu.get_barrier_semaphore()
    for to in partners:
        pl.semaphore_signal(barrier, inc=1, device_id=to, device_id_type=MESH)

    lane = iota((1, LANE), 1)
    row = jnp.full((1, LANE), 64, jnp.int32)
    for p in range(16):
        row = jnp.where(lane == dest_ref[2 * p], off_ref[2 * p] >> 3, row)
    tbl[y, z, q] = row.astype(F32)
    lane = iota((1, 256), 1)
    utterance, step = lane >> 3, lane & 7
    target = jnp.full((1, 256), -1, jnp.int32)
    for u in range(32):
        at = jnp.where(step < len_ref[u], dest_ref[u] * 8 + (off_ref[u] & 7) + step, -1)
        target = jnp.where(utterance == u, at, target)
    place = (iota((256, 256), 0) == target).astype(F32).astype(BF)

    gpv[pl.ds(320, 64), :] = jnp.zeros((64, 512), BF)
    for m in range(4):
        pall[m, pl.ds(320, 64), :] = jnp.zeros((64, 512), BF)

    loads[0].wait()

    @pl.loop(0, 8)
    def _(i):
        rows = xb[pl.ds(pl.multiple_of(i * 128, 128), 128), :].astype(F32)
        for j in range(4):
            xf[j] = rows[:, j * LANE : (j + 1) * LANE]
        for k in range(4):
            part = jnp.concatenate([xf[j, pl.ds(k, 32, stride=4), :] for j in range(4)], axis=1)
            act[pl.ds(pl.multiple_of((k // 2) * 256 + i * 32, 32), 32), (k % 2) * 512 : (k % 2) * 512 + 512] = part.astype(BF)

    pl.semaphore_wait(barrier, len(partners))

    sends = []

    def launch(copy):
        copy.start()
        sends.append(copy)

    for k in range(1, 4):
        launch(remote(tbl.at[y, z, q], tbl.at[y, z, q], idx_s.at[k - 1], idx_r.at[0], (((z + k) % 4) * 8 + q, y)))
    loads[2].wait()
    own, others = pl.multiple_of(c * 160, 160), pl.multiple_of(160 - c * 160, 160)
    up, down, far = (y + 1) % 4, (y + 3) % 4, (y + 2) % 4
    launch(remote(pall.at[y, pl.ds(own, 160)], pall.at[y, pl.ds(own, 160)], ag_s.at[0], ag_r.at[0], (dp, up)))
    launch(remote(pall.at[y, pl.ds(own, 160)], pall.at[y, pl.ds(own, 160)], ag_s.at[1], ag_r.at[1], (dp, down)))

    loads[1].wait()
    pre[...] = dot(act[...], wv[0])

    await_bytes(tbl.at[y, pl.ds(0, 3), 0], idx_r.at[0])
    for k in range(1, 8):
        launch(remote(tbl.at[y, :, q], tbl.at[y, :, q], idx_s.at[2 + k], idx_r.at[1], (z * 8 + (q + k) % 8, y)))

    def norm_gelu(source, gain, shift, xhat, der, rstd, start, count):
        v = source[pl.ds(start, count), :]
        mean = jnp.mean(v, axis=-1, keepdims=True)
        centred = v - mean
        spread = jnp.mean(centred * centred, axis=-1, keepdims=True)
        inv = lax.rsqrt(spread + EPSILON)
        normal = centred * inv
        arg = normal * gain + shift
        cdf = 0.5 + 0.5 * lax.erf(arg * (2.0**-0.5))
        xhat[pl.ds(start, count), :] = normal
        der[pl.ds(start, count), :] = cdf + arg * (jnp.exp(-0.5 * arg * arg) * 0.3989422804014327)
        rstd[pl.ds(start, count), :] = jnp.broadcast_to(inv, (count, LANE))
        return arg * cdf

    gain0, shift0 = gain_ref[0:1, :], shift_ref[0:1, :]
    gain1, shift1 = gain_ref[1:2, :], shift_ref[1:2, :]

    def first_rows(lo, hi):
        @pl.loop(lo, hi)
        def _(i):
            start = pl.multiple_of(i * 32, 32)
            for h in range(2):
                out = norm_gelu(pre, gain0, shift0, xhat0, der0, rstd0, pl.multiple_of(start + h * 256, 32), 32)
                hid[pl.ds(start, 32), h * 512 : (h + 1) * 512] = out.astype(BF)

    first_rows(0, 8)
    pre[pl.ds(0, 256), :] = dot(hid[...], wv[1])

    @pl.loop(0, 4)
    def _(i):
        for h in range(2):
            start = pl.multiple_of(i * 64 + h * 32, 32)
            out = norm_gelu(pre, gain1, shift1, xhat1, der1, rstd1, start, 32)
            frm[pl.ds(start, 32), :] = out.astype(BF)

    fsend[...] = dot(place, frm[...]).astype(BF).reshape(32, 8, 512)

    await_bytes(tbl.at[y, :, pl.ds(0, 7)], idx_r.at[1])
    for k in range(1, 4):
        launch(remote(tbl.at[y], tbl.at[y], idx_s.at[9 + k], idx_r.at[2], (dp, (y + k) % 4)))
    own_f = pltpu.make_async_copy(fsend.at[dp], frecv.at[dp, y], a2a_r.at[1])
    own_f.start()

    @pl.loop(1, 32)
    def _(k):
        to = (dp + k) % 32
        remote(fsend.at[to], frecv.at[dp, y], a2a_s.at[1], a2a_r.at[1], (to, y)).start()

    first, last = pl.multiple_of(own, 16), pl.multiple_of(own + 80, 16)
    await_bytes(pall.at[down, pl.ds(own, 160)], ag_r.at[0])
    launch(remote(pall.at[down, pl.ds(first, 80)], pall.at[down, pl.ds(first, 80)], ag_s.at[2], ag_r.at[2], (dp, up)))
    await_bytes(pall.at[up, pl.ds(own, 160)], ag_r.at[1])
    launch(remote(pall.at[up, pl.ds(last, 80)], pall.at[up, pl.ds(last, 80)], ag_s.at[3], ag_r.at[3], (dp, down)))

    loads[3].wait()
    await_bytes(tbl.at[pl.ds(0, 3)], idx_r.at[2])
    table = jnp.concatenate([tbl[m].reshape(32, LANE) for m in range(4)], axis=0).astype(BF)
    pick = (iota((128, 512), 0) == dp).astype(F32).astype(BF)
    blocks = dot(table, pick).astype(BF)
    row_id = iota((256, 512), 0)
    column = (iota((256, 512), 1) - (row_id & 7)).astype(F32)

    own_g = pltpu.make_async_copy(gsend.at[d], grecv.at[y, dp], a2a_r.at[0])
    for turn in (2, 1, 3, 0):
        part = (z + turn) % 4
        slot = (iota((256, 128), 0) >> 3) + part * 32
        spread = ((slot & 3) * 32 + (slot >> 2) == iota((256, 128), 1)).astype(F32).astype(BF)
        one_hot = (dot(spread, blocks) * 8.0 == column).astype(F32).astype(BF)
        query[pl.ds(pl.multiple_of(part * 256, 256), 256), :] = one_hot
        gsend[pl.ds(part * 32, 32)] = dot(one_hot, gpv[...], NT).astype(BF).reshape(32, 8, WIDE)
        for along in (2, 1, 3, 0):
            for core in range(2):
                to = part * 8 + ((x + along) % 4) * 2 + (c + core) % 2
                for across in (2, 1, 3, 0):
                    side = (y + across) % 4
                    if turn or along or core or across:
                        remote(gsend.at[to * 4 + side], grecv.at[y, dp], a2a_s.at[0], a2a_r.at[0], (to, side)).start()
                    else:
                        own_g.start()

    await_bytes(pall.at[far, pl.ds(first, 80)], ag_r.at[2])
    await_bytes(pall.at[far, pl.ds(last, 80)], ag_r.at[3])
    mate = (dp_of(z, x, 1 - c), y)
    for n, at in enumerate((up, down, far)):
        launch(remote(pall.at[at, pl.ds(own, 160)], pall.at[at, pl.ds(own, 160)], ag_s.at[4 + n], ag_r.at[4 + n], mate))

    actt[...] = act[...].T
    hidt[...] = hid[...].T
    for n, at in enumerate((up, down, far)):
        await_bytes(pall.at[at, pl.ds(others, 160)], ag_r.at[4 + n])
    await_bytes(frecv.at[:, 0], a2a_r.at[1])
    await_bytes(grecv, a2a_r.at[0])
    low, high = pl.ds(0, 16), pl.ds(16, 16)
    for n, (to, half) in enumerate(((up, low), (down, high), (up, high), (down, low))):
        launch(remote(frecv.at[half, y], frecv.at[half, y], fg_s.at[n], fg_r.at[n], (dp, to)))

    total = None
    for m in range(4):
        part = dot(grecv[m].reshape(256, WIDE), pall[m])
        total = part if total is None else total + part
    grad_frames = dot(place, total.astype(BF), TN)
    gh[pl.ds(0, 256), :] = grad_frames

    sizes = dict(x=x, y=y, z=z)

    def peer(axis, k):
        if axis == "x":
            return (dp_of(z, (x + k) % 4, c), y)
        if axis == "z":
            return (dp_of((z + k) % 4, x, c), y)
        return (dp, (y + k) % 4)

    def chunk(ref, lead, dims, axis, at):
        pos = dims.index(axis)
        return ref.at[tuple(lead) + (slice(None),) * pos + (at,)]

    def scatter(source, landing, lead, dims, axis, sem):
        for k in range(1, 4):
            at = (sizes[axis] + k) % 4
            launch(
                remote(
                    chunk(source, lead, dims, axis, at),
                    landing.at[tuple(lead) + (k - 1,)],
                    rs_s.at[sem, k - 1],
                    rs_r.at[sem],
                    peer(axis, k),
                )
            )

    def gather(source, landing, lead, dims, axis, sem):
        await_bytes(landing.at[tuple(lead) + (pl.ds(0, 3),)], rs_r.at[sem])
        total = chunk(source, lead, dims, axis, sizes[axis])[...].astype(F32)
        for k in range(3):
            total = total + landing[tuple(lead) + (k,)].astype(F32)
        return total

    def norm_back(upstream, gain, xhat, der, rstd, start, count, sums):
        dy = upstream * der[pl.ds(start, count), :]
        normal = xhat[pl.ds(start, count), :]
        dyn = dy * normal
        dg = sums[0] + dyn.reshape(count // 8, 8, 512).sum(axis=0)
        ds = sums[1] + dy.reshape(count // 8, 8, 512).sum(axis=0)
        mean_d = jnp.mean(dy * gain, axis=-1, keepdims=True)
        mean_dn = jnp.mean(dyn * gain, axis=-1, keepdims=True)
        inv = rstd[pl.ds(start, count), :][:, 0:1]
        return inv * (dy * gain - mean_d - normal * mean_dn), (dg, ds)

    def put_norm(layer, sums):
        for half in range(2):
            row = sums[half].sum(axis=0, keepdims=True)
            for j in range(4):
                nrm[layer * 8 + half * 4 + j : layer * 8 + half * 4 + j + 1, :] = row[:, j * LANE : (j + 1) * LANE]

    zeros = (jnp.zeros((8, 512), F32), jnp.zeros((8, 512), F32))

    def second_body(i, sums):
        for h in range(2):
            start = pl.multiple_of(i * 64 + h * 32, 32)
            out, sums = norm_back(gh[pl.ds(start, 32), :], gain1, xhat1, der1, rstd1, start, 32, sums)
            gf[pl.ds(start, 32), :] = out.astype(BF)
        return sums

    sums1 = lax.fori_loop(0, 4, second_body, zeros)
    put_norm(1, sums1)
    grad_second = gf[pl.ds(0, 256), :]
    for h in range(2):
        gh[pl.ds(h * 256, 256), :] = dot(grad_second, wv[1, pl.ds(h * 512, 512), :], NT).astype(BF).astype(F32)

    def forward_frames():
        await_bytes(frecv.at[low, down], fg_r.at[0])
        launch(remote(frecv.at[low, down], frecv.at[low, down], fg_s.at[4], fg_r.at[4], (dp, up)))
        await_bytes(frecv.at[high, up], fg_r.at[1])
        launch(remote(frecv.at[high, up], frecv.at[high, up], fg_s.at[5], fg_r.at[5], (dp, down)))

    def kernel_grad(layer, left, sem):
        for half in range(2):
            right = gf[0 : left.shape[1], half * 256 : half * 256 + 256]
            for h in range(4):
                part = dot(left[h * 256 : (h + 1) * 256, :], right).astype(BF)
                for j in range(2):
                    convp[layer, 2 * half + j, h] = part[:, j * LANE : (j + 1) * LANE].reshape(4, 2, 4, 8, LANE)
            for j in (2 * half, 2 * half + 1):
                launch(remote(convp.at[layer, j, :, :, 1 - c], convr.at[layer, j], rs_s.at[sem + j, 3], rs_r.at[sem + j], mate))

    kernel_grad(1, hidt, 0)

    def conv_core(layer, j, sem):
        await_bytes(convr.at[layer, j], rs_r.at[sem])
        convb[layer, j] = (
            convp[layer, j, :, :, c].astype(F32) + convr[layer, j].astype(F32)
        ).astype(BF)

    base = ("z", "x", "y")
    plane = sorted([(i, j) for i in range(4) for j in range(4) if i or j], key=lambda one: one.count(2) * 5 + 4 - one.count(0), reverse=True)

    def conv_send(layer, j, sem):
        scatter(convb, conv1, (layer, j), base, ("x", "z")[j % 2], sem)

    def conv_take(layer, j, sem):
        total = gather(convb, conv1, (layer, j), base, ("x", "z")[j % 2], sem)
        convb1[j % 2, :, :, layer, j // 2] = total.astype(BF)

    def plane_peer(axis, i, j):
        if axis == "z":
            return (dp_of((z + i) % 4, x, c), (y + j) % 4)
        return (dp_of(z, (x + i) % 4, c), (y + j) % 4)

    def conv_last_send(p):
        axis = ("z", "x")[p]
        for n, (i, j) in enumerate(plane):
            launch(
                remote(
                    convb1.at[p, (sizes[axis] + i) % 4, (y + j) % 4],
                    conv2.at[p, n],
                    pl_s.at[p, n],
                    pl_r.at[p],
                    plane_peer(axis, i, j),
                )
            )

    def conv_last_take(p):
        await_bytes(conv2.at[p], pl_r.at[p])
        total = convb1[p, sizes[("z", "x")[p]], y].astype(F32)
        for n in range(15):
            total = total + conv2[p, n].astype(F32)
        for layer in range(2):
            for j in range(2):
                at = 2 * j + p
                gconv_out[layer, :, at * LANE : (at + 1) * LANE] = total[layer, j]

    def first_body(i, sums):
        for h in range(2):
            start = pl.multiple_of(i * 64 + h * 32, 32)
            out, sums = norm_back(gh[pl.ds(start, 32), :], gain0, xhat0, der0, rstd0, start, 32, sums)
            gf[pl.ds(start, 32), :] = out.astype(BF)
        return sums

    sums0 = lax.fori_loop(0, 8, first_body, zeros)
    put_norm(0, sums0)
    to_mate = remote(nrm, nrmr, nm_s.at[0, 0], nm_r.at[0], mate)
    to_mate.start()

    for j in range(4):
        conv_core(1, j, j)
        conv_send(1, j, 16 + j)
    kernel_grad(0, actt, 8)
    forward_frames()
    await_bytes(nrmr, nm_r.at[0])
    to_mate.wait_send()
    nrm[...] = nrm[...] + nrmr[...]
    moving = []
    for k in range(1, 4):
        moving.append(remote(nrm, nrm1.at[k - 1], nm_s.at[1, k - 1], nm_r.at[1], peer("x", k)))
        moving[-1].start()
    for j in range(4):
        conv_core(0, j, 8 + j)
        conv_send(0, j, 20 + j)

    for h in range(2):
        gx[pl.ds(h * 256, 256), :] = dot(gf[pl.ds(h * 256, 256), :], wv[0], NT)

    @pl.loop(0, 8)
    def _(i):
        for h in range(2):
            rows = gx[pl.ds(pl.multiple_of(h * 256 + i * 32, 32), 32), :]
            for k in range(2):
                for j in range(4):
                    xo[j, pl.ds(2 * h + k, 32, stride=4), :] = rows[:, k * 512 + j * LANE : k * 512 + (j + 1) * LANE]
        out = jnp.concatenate([xo[j] for j in range(4)], axis=1)
        gfeat_out[pl.ds(pl.multiple_of(i * 128, 128), 128), :] = out.astype(BF)

    for j in range(4):
        conv_take(1, j, 16 + j)
    await_bytes(nrm1, nm_r.at[1])
    for one in moving:
        one.wait_send()
    nrm[...] = nrm[...] + nrm1[0] + nrm1[1] + nrm1[2]
    for n, (i, j) in enumerate(plane):
        launch(remote(nrm, nrm2.at[n], pl_s.at[2, n], pl_r.at[2], plane_peer("z", i, j)))

    await_bytes(frecv.at[high, down], fg_r.at[2])
    await_bytes(frecv.at[low, up], fg_r.at[3])
    await_bytes(frecv.at[low, far], fg_r.at[4])
    await_bytes(frecv.at[high, far], fg_r.at[5])
    packin[...] = dot(frecv[...].reshape(1024, 512), query[...], TN).astype(BF)
    part = dot(packin[...], gpv[...], NT).astype(BF)
    projp[...] = part.reshape(4, 4, 2, 16, WIDE)
    launch(remote(projp.at[:, :, 1 - c], projr, rs_s.at[4, 3], rs_r.at[4], mate))
    packed_out[...] = dot(pall[y, pl.ds(0, 320), :], packin[...]).astype(BF)
    for j in (0, 2):
        conv_take(0, j, 20 + j)
    conv_last_send(0)
    for j in (1, 3):
        conv_take(0, j, 20 + j)
    conv_last_send(1)
    await_bytes(projr, rs_r.at[4])
    projb[...] = (projp[:, :, c].astype(F32) + projr[...].astype(F32)).astype(BF)
    for n, (i, j) in enumerate(plane):
        launch(
            remote(
                projb.at[(z + i) % 4, (x + j) % 4],
                proj1.at[n],
                pl_s.at[3, n],
                pl_r.at[3],
                (dp_of((z + i) % 4, (x + j) % 4, c), y),
            )
        )
    await_bytes(nrm2, pl_r.at[2])
    total = nrm[...]
    for n in range(15):
        total = total + nrm2[n]
    gnorm_out[...] = total
    for p in range(2):
        conv_last_take(p)
    await_bytes(proj1, pl_r.at[3])
    total = projb[z, x].astype(F32)
    for n in range(15):
        total = total + proj1[n].astype(F32)
    gproj_out[...] = total[:, 0:320]

    for one in sends:
        one.wait_send()
    await_bytes(gsend.at[pl.ds(0, 127)], a2a_s.at[0])
    await_bytes(fsend.at[pl.ds(0, 31)], a2a_s.at[1])


def finish(
    packed_in, gfeat_in, gconv_in, gproj_in, gnorm_in, packed_out, gfeat_out, gconv_out, gproj_out, gnorm_out, sem
):
    copies = [
        pltpu.make_async_copy(packed_in, packed_out, sem.at[0]),
        pltpu.make_async_copy(gfeat_in, gfeat_out, sem.at[1]),
        pltpu.make_async_copy(gconv_in, gconv_out, sem.at[2]),
        pltpu.make_async_copy(gproj_in, gproj_out, sem.at[3]),
    ]
    for one in (1, 0, 2, 3):
        copies[one].start()
    d = lax.axis_index("dp") * 4 + lax.axis_index("mp")
    for layer in range(2):
        row = gnorm_in[pl.ds(layer * 8 + d // 16, 1), :]
        turned = pltpu.roll(row, LANE - (d % 16) * 8, 1)
        gnorm_out[layer : layer + 1, :] = turned[:, 0:8]
    for one in copies:
        one.wait()


def local(features, lengths, dests, offsets, conv_weight, norm_gain, norm_shift, proj_weight, grad_packed):
    vmem = pl.BlockSpec(memory_space=pltpu.VMEM)
    hbm = pl.BlockSpec(memory_space=pltpu.HBM)
    smem = pl.BlockSpec(memory_space=pltpu.SMEM)
    V = pltpu.VMEM
    D = pltpu.SemaphoreType.DMA
    scratch = [
        V((1024, 512), BF), V((2, 1024, 512), BF), V((WIDE, 512), BF), V((4, 128, LANE), F32),
        V((512, 1024), BF), V((1024, 512), BF), V((512, 512), F32), V((512, 512), F32), V((512, 512), F32), V((512, LANE), F32),
        V((256, 512), F32), V((256, 512), F32), V((256, LANE), F32),
        V((256, 1024), BF), V((1024, 256), BF), V((256, 512), BF),
        V((4, 4, 8, 1, LANE), F32), V((1024, 512), BF), V((128, 8, WIDE), BF), V((4, 32, 8, WIDE), BF),
        V((32, 8, 512), BF), V((32, 4, 8, 512), BF), V((4, WIDE, 512), BF), V((512, 512), BF),
        V((512, 512), F32), V((512, 512), BF), V((512, 1024), F32), V((4, 128, LANE), F32),
        V((2, 4, 4, 4, 2, 4, 8, LANE), BF), V((2, 4, 4, 4, 4, 8, LANE), BF), V((2, 4, 4, 4, 4, 8, LANE), BF),
        V((2, 4, 3, 4, 4, 8, LANE), BF), V((2, 4, 4, 2, 2, 8, LANE), BF), V((2, 15, 2, 2, 8, LANE), BF),
        V((4, 4, 2, 16, WIDE), BF), V((4, 4, 16, WIDE), BF), V((4, 4, 16, WIDE), BF), V((15, 16, WIDE), BF),
        V((16, LANE), F32), V((16, LANE), F32), V((3, 16, LANE), F32), V((15, 16, LANE), F32),
        D((4,)), D((13,)), D((3,)), D((7,)), D((7,)), D((2,)), D((2,)), D((6,)), D((6,)), D((24, 4)), D((24,)), D((2, 3)), D((2,)), D((4, 15)), D((4,)),
    ]
    results = ((320, 512), BF), ((1024, 512), BF), ((2, 8, 512), F32), ((16, 320), F32), ((16, LANE), F32)
    middle = pl.pallas_call(
        kernel,
        out_shape=tuple(pltpu.VMEM(*one) for one in results),
        in_specs=[smem] * 3 + [vmem] * 2 + [hbm] * 4,
        out_specs=(vmem,) * 5,
        scratch_shapes=scratch,
        compiler_params=pltpu.CompilerParams(collective_id=0, has_side_effects=True, vmem_limit_bytes=65_400_000),
    )(
        lengths, dests, offsets, norm_gain, norm_shift, features.reshape(1024, 512), conv_weight,
        proj_weight.T, grad_packed.T,
    )
    shapes = (*results[:4], ((2, 8), F32))
    packed, gfeat, gconv, gproj, gnorm = pl.pallas_call(
        finish,
        out_shape=tuple(jax.ShapeDtypeStruct(*one) for one in shapes),
        in_specs=[vmem] * 5,
        out_specs=(hbm, hbm, hbm, hbm, vmem),
        scratch_shapes=[D((4,))],
    )(*[pltpu.with_memory_space_constraint(one, pltpu.VMEM) for one in middle])
    return packed.T, gfeat.reshape(32, 32, 512), gconv, gnorm, gproj


def solution(mesh):
    return jax.shard_map(
        local,
        mesh=mesh,
        in_specs=(
            P(("dp", "mp"), None, None),
            P(("dp", "mp")),
            P(("dp", "mp")),
            P(("dp", "mp")),
            P(),
            P(),
            P(),
            P(None, "mp"),
            P("dp", "mp"),
        ),
        out_specs=(
            P("dp", "mp"),
            P(("dp", "mp"), None, None),
            P(None, ("dp", "mp"), None),
            P(None, ("dp", "mp")),
            P("dp", "mp"),
        ),
        check_vma=False,
    )
```

```python
import jax
import jax.numpy as jnp
from jax import lax
from jax.experimental import pallas as pl
from jax.experimental.pallas import tpu as pltpu
from jax.sharding import PartitionSpec as P

EPSILON = 1e-05
BF = jnp.bfloat16
F32 = jnp.float32
MESH = pl.DeviceIdType.MESH
NN = (((1,), (0,)), ((), ()))
NT = (((1,), (1,)), ((), ()))
TN = (((0,), (0,)), ((), ()))
LANE = 128
WIDE = 384


def dot(a, b, dims=NN):
    return lax.dot_general(a, b, dims, preferred_element_type=F32)


def iota(shape, dim):
    return lax.broadcasted_iota(jnp.int32, shape, dim)


def kernel(
    len_hbm, dest_hbm, off_hbm, gain_hbm, shift_hbm, feat_hbm, weight_hbm, proj_hbm, gp_hbm,
    packed_out, gfeat_out, gconv_out, gproj_out, gnorm_out,
    len_ref, dest_ref, off_ref, gain_ref, shift_ref, xb, wv, gpv, gpe, xf, act, actt, placet, pre, xhat0, der0, rstd0, xhat1, der1, rstd1, hid, hidt, frm,
    tbl, query, gsendb, gsends, gbig, gsmall, fsend, frecv, pall, packin,
    gh, gf, gx, xo,
    convp, convr, convb, conv1, convb1, conv2,
    projp, projr, projb, proj1,
    nrm, nrmr, nrm1, nrm2,
    in_sem, idx_s, idx_r, ag_s, ag_r, g_s, g_r, a2a_s, a2a_r, fg_s, fg_r, rs_s, rs_r, nm_s, nm_r, pl_s, pl_r,
):
    dp = lax.axis_index("dp")
    y = lax.axis_index("mp")
    z, q = dp // 8, dp % 8
    x, c = q // 2, q % 2
    odd = y % 2
    mine = (y // 2, pl.multiple_of(odd * 320, 64))

    def dp_of(zz, xx, cc):
        return zz * 8 + xx * 2 + cc

    def remote(src, dst, ssem, rsem, to):
        return pltpu.make_async_remote_copy(
            src_ref=src, dst_ref=dst, send_sem=ssem, recv_sem=rsem, device_id=to, device_id_type=MESH
        )

    def await_bytes(ref, sem):
        pltpu.make_async_copy(ref, ref, sem).wait()

    loads = [
        pltpu.make_async_copy(feat_hbm, xb, in_sem.at[0]),
        pltpu.make_async_copy(weight_hbm, wv, in_sem.at[1]),
        pltpu.make_async_copy(proj_hbm, pall.at[mine[0], pl.ds(mine[1], 320)], in_sem.at[2]),
        pltpu.make_async_copy(gp_hbm, gpv.at[pl.ds(0, 320)], in_sem.at[3]),
        pltpu.make_async_copy(gp_hbm, gpe.at[pl.ds(pl.multiple_of(odd * 64, 64), 320)], in_sem.at[4]),
    ]
    partners = (
        [(dp, (y + k) % 4) for k in range(1, 4)]
        + [(z * 8 + (q + k) % 8, y) for k in range(1, 8)]
        + [(((z + k) % 4) * 8 + q, y) for k in range(1, 4)]
    )
    barrier = pltpu.get_barrier_semaphore()
    for to in partners:
        pl.semaphore_signal(barrier, inc=1, device_id=to, device_id_type=MESH)
    small = [
        pltpu.make_async_copy(source, target, in_sem.at[5 + n])
        for n, (source, target) in enumerate(
            ((len_hbm, len_ref), (dest_hbm, dest_ref), (off_hbm, off_ref), (gain_hbm, gain_ref), (shift_hbm, shift_ref))
        )
    ]
    for one in small:
        one.start()
    for one in (0, 2, 4, 1, 3):
        loads[one].start()
    for one in small:
        one.wait()

    lane = iota((1, LANE), 1)
    row = jnp.full((1, LANE), 64, jnp.int32)
    for p in range(16):
        row = jnp.where(lane == dest_ref[2 * p], off_ref[2 * p] >> 3, row)
    tbl[y, z, q] = row.astype(F32)
    lane = iota((1, 256), 1)
    utterance, step = lane >> 3, lane & 7
    target = jnp.full((1, 256), -1, jnp.int32)
    for u in range(32):
        at = jnp.where(step < len_ref[u], dest_ref[u] * 8 + (off_ref[u] & 7) + step, -1)
        target = jnp.where(utterance == u, at, target)
    place = (iota((256, 256), 0) == target).astype(F32).astype(BF)

    gpv[pl.ds(320, 64), :] = jnp.zeros((64, 512), BF)

    loads[0].wait()

    @pl.loop(0, 8)
    def _(i):
        rows = xb[pl.ds(pl.multiple_of(i * 128, 128), 128), :].astype(F32)
        for j in range(4):
            xf[j] = rows[:, j * LANE : (j + 1) * LANE]
        for k in range(4):
            part = jnp.concatenate([xf[j, pl.ds(k, 32, stride=4), :] for j in range(4)], axis=1)
            act[pl.ds(pl.multiple_of((k // 2) * 256 + i * 32, 32), 32), (k % 2) * 512 : (k % 2) * 512 + 512] = part.astype(BF)

    pl.semaphore_wait(barrier, len(partners))

    sends = []

    def launch(copy):
        copy.start()

    def sent(ref, sem):
        sends.append((ref, sem))

    for k in range(1, 4):
        launch(remote(tbl.at[y, z, q], tbl.at[y, z, q], idx_s.at[0], idx_r.at[0], (((z + k) % 4) * 8 + q, y)))
    loads[2].wait()
    up, down, far = (y + 1) % 4, (y + 3) % 4, (y + 2) % 4

    def shard(yy, start, count):
        at = pl.multiple_of((yy % 2) * 320 + start, 16)
        return pall.at[yy // 2, pl.ds(at, count)]

    own = c * 160
    launch(remote(shard(y, own, 160), shard(y, own, 160), ag_s.at[0], ag_r.at[0], (dp, up)))
    launch(remote(shard(y, own, 160), shard(y, own, 160), ag_s.at[0], ag_r.at[1], (dp, down)))
    sent(pall.at[0, pl.ds(0, 320)], ag_s.at[0])
    loads[4].wait()
    edge = gpe.at[pl.ds(pl.multiple_of(256 - 192 * odd, 64), 64)]
    launch(remote(edge, gpe.at[pl.ds(pl.multiple_of(320 * odd, 64), 64)], ag_s.at[3], ag_r.at[4], (dp, y + 1 - 2 * odd)))
    sent(edge, ag_s.at[3])

    loads[1].wait()
    pre[...] = dot(act[...], wv[0])

    await_bytes(tbl.at[y, pl.ds(0, 3), 0], idx_r.at[0])
    sent(tbl.at[y, pl.ds(0, 3), 0], idx_s.at[0])
    for k in range(1, 8):
        launch(remote(tbl.at[y, :, q], tbl.at[y, :, q], idx_s.at[1], idx_r.at[1], (z * 8 + (q + k) % 8, y)))

    def norm_gelu(source, gain, shift, xhat, der, rstd, start, count):
        v = source[pl.ds(start, count), :]
        mean = jnp.mean(v, axis=-1, keepdims=True)
        centred = v - mean
        spread = jnp.mean(centred * centred, axis=-1, keepdims=True)
        inv = lax.rsqrt(spread + EPSILON)
        normal = centred * inv
        arg = normal * gain + shift
        cdf = 0.5 + 0.5 * lax.erf(arg * (2.0**-0.5))
        xhat[pl.ds(start, count), :] = normal
        der[pl.ds(start, count), :] = cdf + arg * (jnp.exp(-0.5 * arg * arg) * 0.3989422804014327)
        rstd[pl.ds(start, count), :] = jnp.broadcast_to(inv, (count, LANE))
        return arg * cdf

    gain0, shift0 = gain_ref[0:1, :], shift_ref[0:1, :]
    gain1, shift1 = gain_ref[1:2, :], shift_ref[1:2, :]

    def first_rows(lo, hi):
        @pl.loop(lo, hi)
        def _(i):
            start = pl.multiple_of(i * 32, 32)
            for h in range(2):
                out = norm_gelu(pre, gain0, shift0, xhat0, der0, rstd0, pl.multiple_of(start + h * 256, 32), 32)
                hid[pl.ds(start, 32), h * 512 : (h + 1) * 512] = out.astype(BF)

    first_rows(0, 8)
    pre[pl.ds(0, 256), :] = dot(hid[...], wv[1])

    @pl.loop(0, 4)
    def _(i):
        for h in range(2):
            start = pl.multiple_of(i * 64 + h * 32, 32)
            out = norm_gelu(pre, gain1, shift1, xhat1, der1, rstd1, start, 32)
            frm[pl.ds(start, 32), :] = out.astype(BF)

    fsend[...] = dot(place, frm[...]).astype(BF).reshape(32, 8, 512)

    await_bytes(tbl.at[y, :, pl.ds(0, 7)], idx_r.at[1])
    sent(tbl.at[y, :, pl.ds(0, 7)], idx_s.at[1])
    for k in range(1, 4):
        launch(remote(tbl.at[y], tbl.at[y], idx_s.at[2], idx_r.at[2], (dp, (y + k) % 4)))
    own_f = pltpu.make_async_copy(fsend.at[dp], frecv.at[dp, y], a2a_r.at[0])
    own_f.start()

    @pl.loop(1, 32)
    def _(k):
        to = (dp + k) % 32
        remote(fsend.at[to], frecv.at[dp, y], a2a_s.at[0], a2a_r.at[0], (to, y)).start()

    await_bytes(shard(down, own, 160), ag_r.at[0])
    launch(remote(shard(down, own, 80), shard(down, own, 80), ag_s.at[1], ag_r.at[2], (dp, up)))
    await_bytes(shard(up, own, 160), ag_r.at[1])
    launch(remote(shard(up, own + 80, 80), shard(up, own + 80, 80), ag_s.at[1], ag_r.at[2], (dp, down)))
    sent(shard(y, 0, 160), ag_s.at[1])

    loads[3].wait()
    await_bytes(tbl.at[pl.ds(0, 3)], idx_r.at[2])
    sent(tbl.at[pl.ds(0, 3)], idx_s.at[2])
    table = jnp.concatenate([tbl[m].reshape(32, LANE) for m in range(4)], axis=0).astype(BF)
    pick = (iota((128, 512), 0) == dp).astype(F32).astype(BF)
    blocks = dot(table, pick).astype(BF)
    row_id = iota((128, 512), 0)
    column = (iota((128, 512), 1) - (row_id & 7)).astype(F32)
    slot = iota((128, 128), 0) >> 3
    wanted = (slot & 3) * 32 + (slot >> 2) * 2
    await_bytes(gpe.at[pl.ds(0, 64)], ag_r.at[4])

    for turn in (2, 1, 3, 0):
        part = (z + turn) % 4
        for kind in range(2):
            core = odd if kind == 0 else 1 - odd
            spread = (wanted + part * 8 + core == iota((128, 128), 1)).astype(F32).astype(BF)
            one_hot = (dot(spread, blocks) * 8.0 == column).astype(F32).astype(BF)
            if kind == 0:
                values = dot(one_hot, gpe[...], NT)
                gsendb[pl.ds(part * 16, 16)] = values.astype(BF).reshape(16, 8, 384)
            else:
                values = dot(one_hot, gpe[pl.ds(pl.multiple_of(128 * odd, 128), 256), :], NT)
                gsends[pl.ds(part * 16, 16)] = values.astype(BF).reshape(16, 8, 256)
        for along in (2, 1, 3, 0):
            for across in (2, 1, 3, 0):
                side = (y + across) % 4
                column_x = (x + along) % 4
                for kind, (source, landing) in enumerate(((gsendb, gbig), (gsends, gsmall))):
                    core = odd if kind == 0 else 1 - odd
                    src = source.at[part * 16 + column_x * 4 + side]
                    dst = landing.at[y // 2, dp]
                    copy = remote(src, dst, g_s.at[kind], g_r.at[kind], (dp_of(part, column_x, core), side))
                    if turn or along or across:
                        copy.start()
                    else:
                        pl.when(core != c)(copy.start)
                        pl.when(core == c)(pltpu.make_async_copy(src, dst, g_r.at[kind]).start)

    await_bytes(shard(far, own, 160), ag_r.at[2])
    mate = (dp_of(z, x, 1 - c), y)
    for at in (up, down, far):
        launch(remote(shard(at, own, 160), shard(at, own, 160), ag_s.at[2], ag_r.at[3], mate))
    sent(pall.at[0, pl.ds(0, 480)], ag_s.at[2])

    placet[...] = place.T
    for part in range(4):
        slot = (iota((256, 128), 0) >> 3) + part * 32
        spread = ((slot & 3) * 32 + (slot >> 2) == iota((256, 128), 1)).astype(F32).astype(BF)
        column = (iota((256, 512), 1) - (iota((256, 512), 0) & 7)).astype(F32)
        query[part * 256 : part * 256 + 256, :] = (dot(spread, blocks) * 8.0 == column).astype(F32).astype(BF)
    actt[...] = act[...].T
    hidt[...] = hid[...].T
    await_bytes(pall.at[0, pl.ds(0, 480)], ag_r.at[3])
    await_bytes(frecv.at[:, 0], a2a_r.at[0])
    low, high = pl.ds(0, 16), pl.ds(16, 16)
    for n, (to, half) in enumerate(((up, low), (down, high), (up, high), (down, low))):
        launch(remote(frecv.at[half, y], frecv.at[half, y], fg_s.at[0], fg_r.at[min(n, 2)], (dp, to)))
    sent(frecv.at[low], fg_s.at[0])
    await_bytes(gbig, g_r.at[0])
    await_bytes(gsmall, g_r.at[1])

    total = None
    for m in range(2):
        part = dot(gbig[m].reshape(256, 384), pall[m, pl.ds(pl.multiple_of(256 * c, 128), 384), :])
        total = part if total is None else total + part
        total = total + dot(gsmall[m].reshape(256, 256), pall[m, pl.ds(pl.multiple_of(384 - 384 * c, 128), 256), :])
    grad_frames = dot(placet[...], total.astype(BF))
    gh[pl.ds(0, 256), :] = grad_frames

    sizes = dict(x=x, y=y, z=z)

    def peer(axis, k):
        if axis == "x":
            return (dp_of(z, (x + k) % 4, c), y)
        if axis == "z":
            return (dp_of((z + k) % 4, x, c), y)
        return (dp, (y + k) % 4)

    def chunk(ref, lead, dims, axis, at):
        pos = dims.index(axis)
        return ref.at[tuple(lead) + (slice(None),) * pos + (at,)]

    def scatter(source, landing, lead, dims, axis, send, sem):
        for k in range(1, 4):
            at = (sizes[axis] + k) % 4
            launch(
                remote(
                    chunk(source, lead, dims, axis, at),
                    landing.at[tuple(lead) + (k - 1,)],
                    rs_s.at[send],
                    rs_r.at[sem],
                    peer(axis, k),
                )
            )

    def gather(source, landing, lead, dims, axis):
        total = chunk(source, lead, dims, axis, sizes[axis])[...].astype(F32)
        for k in range(3):
            total = total + landing[tuple(lead) + (k,)].astype(F32)
        return total

    def norm_back(upstream, gain, xhat, der, rstd, start, count, sums):
        dy = upstream * der[pl.ds(start, count), :]
        normal = xhat[pl.ds(start, count), :]
        dyn = dy * normal
        dg = sums[0] + dyn.reshape(count // 8, 8, 512).sum(axis=0)
        ds = sums[1] + dy.reshape(count // 8, 8, 512).sum(axis=0)
        mean_d = jnp.mean(dy * gain, axis=-1, keepdims=True)
        mean_dn = jnp.mean(dyn * gain, axis=-1, keepdims=True)
        inv = rstd[pl.ds(start, count), :][:, 0:1]
        return inv * (dy * gain - mean_d - normal * mean_dn), (dg, ds)

    def put_norm(layer, sums):
        for half in range(2):
            row = sums[half].sum(axis=0, keepdims=True)
            for j in range(4):
                nrm[layer * 8 + half * 4 + j : layer * 8 + half * 4 + j + 1, :] = row[:, j * LANE : (j + 1) * LANE]

    zeros = (jnp.zeros((8, 512), F32), jnp.zeros((8, 512), F32))

    def second_body(i, sums):
        for h in range(2):
            start = pl.multiple_of(i * 64 + h * 32, 32)
            out, sums = norm_back(gh[pl.ds(start, 32), :], gain1, xhat1, der1, rstd1, start, 32, sums)
            gf[pl.ds(start, 32), :] = out.astype(BF)
        return sums

    sums1 = lax.fori_loop(0, 4, second_body, zeros)
    put_norm(1, sums1)
    grad_second = gf[pl.ds(0, 256), :]
    for h in range(2):
        gh[pl.ds(h * 256, 256), :] = dot(grad_second, wv[1, pl.ds(h * 512, 512), :], NT).astype(BF).astype(F32)

    def forward_frames():
        await_bytes(frecv.at[low, down], fg_r.at[0])
        launch(remote(frecv.at[low, down], frecv.at[low, down], fg_s.at[1], fg_r.at[2], (dp, up)))
        await_bytes(frecv.at[high, up], fg_r.at[1])
        launch(remote(frecv.at[high, up], frecv.at[high, up], fg_s.at[1], fg_r.at[2], (dp, down)))
        sent(frecv.at[:, y], fg_s.at[1])

    def kernel_grad(layer, left):
        for half in range(2):
            right = gf[0 : left.shape[1], half * 256 : half * 256 + 256]
            for h in range(4):
                part = dot(left[h * 256 : (h + 1) * 256, :], right).astype(BF)
                for j in range(2):
                    convp[layer, 2 * half + j, h] = part[:, j * LANE : (j + 1) * LANE].reshape(4, 2, 4, 8, LANE)
            for j in (2 * half, 2 * half + 1):
                launch(remote(convp.at[layer, j, :, :, 1 - c], convr.at[layer, j], rs_s.at[layer], rs_r.at[2 * layer + half], mate))
        sent(convr.at[layer], rs_s.at[layer])

    kernel_grad(1, hidt)
    forward_frames()

    def conv_core(layer, j):
        if j % 2 == 0:
            await_bytes(convr.at[layer, pl.ds(j, 2)], rs_r.at[2 * layer + j // 2])
        convb[layer, j] = (
            convp[layer, j, :, :, c].astype(F32) + convr[layer, j].astype(F32)
        ).astype(BF)

    base = ("z", "x", "y")
    plane = sorted([(i, j) for i in range(4) for j in range(4) if i or j], key=lambda one: one.count(2) * 5 + 4 - one.count(0), reverse=True)

    conv_axis = (("x", "z", "y", "y"), ("x", "z", "x", "z"))
    groups = {
        axis: [(layer, j) for layer in range(2) for j in range(4) if conv_axis[layer][j] == axis] for axis in "xyz"
    }
    order = "xyz"

    def others_of(axis):
        return tuple(one for one in base if one != axis)

    def conv_send(layer, j):
        scatter(convb, conv1, (layer, j), base, conv_axis[layer][j], 3 + layer, 5 if layer else 6 + j)
        if j == 3:
            sent(conv1.at[layer], rs_s.at[3 + layer])

    def conv_take(layer, j):
        axis = conv_axis[layer][j]
        if layer == 0:
            await_bytes(conv1.at[layer, j], rs_r.at[6 + j])
        elif j == 0:
            await_bytes(conv1.at[layer], rs_r.at[5])
        total = gather(convb, conv1, (layer, j), base, axis)
        convb1[order.index(axis), :, :, groups[axis].index((layer, j))] = total.astype(BF)

    def plane_peer(first, second, i, j):
        at = dict(sizes)
        at[first] = (at[first] + i) % 4
        at[second] = (at[second] + j) % 4
        return (dp_of(at["z"], at["x"], c), at["y"])

    def conv_last_send(axis):
        p, count = order.index(axis), len(groups[axis])
        first, second = others_of(axis)
        for n, (i, j) in enumerate(plane):
            launch(
                remote(
                    convb1.at[p, (sizes[first] + i) % 4, (sizes[second] + j) % 4, pl.ds(0, count)],
                    conv2.at[p, n, pl.ds(0, count)],
                    pl_s.at[p],
                    pl_r.at[p],
                    plane_peer(first, second, i, j),
                )
            )
        sent(conv2.at[p, :, pl.ds(0, count)], pl_s.at[p])

    def conv_last_take(axis):
        p, count = order.index(axis), len(groups[axis])
        first, second = others_of(axis)
        await_bytes(conv2.at[p, :, pl.ds(0, count)], pl_r.at[p])
        total = convb1[p, sizes[first], sizes[second], 0:count].astype(F32)
        for n in range(15):
            total = total + conv2[p, n, 0:count].astype(F32)
        for at, (layer, j) in enumerate(groups[axis]):
            gconv_out[layer, :, j * LANE : (j + 1) * LANE] = total[at]

    def first_body(i, sums):
        for h in range(2):
            start = pl.multiple_of(i * 64 + h * 32, 32)
            out, sums = norm_back(gh[pl.ds(start, 32), :], gain0, xhat0, der0, rstd0, start, 32, sums)
            gf[pl.ds(start, 32), :] = out.astype(BF)
        return sums

    sums0 = lax.fori_loop(0, 8, first_body, zeros)
    put_norm(0, sums0)
    to_mate = remote(nrm, nrmr, nm_s.at[0], nm_r.at[0], mate)
    to_mate.start()

    for j in range(4):
        conv_core(1, j)
        conv_send(1, j)
    kernel_grad(0, actt)
    for h in range(2):
        gx[pl.ds(h * 256, 256), :] = dot(gf[pl.ds(h * 256, 256), :], wv[0], NT)
    await_bytes(nrmr, nm_r.at[0])
    to_mate.wait_send()
    nrm[...] = nrm[...] + nrmr[...]
    for k in range(1, 4):
        launch(remote(nrm, nrm1.at[k - 1], nm_s.at[1], nm_r.at[1], peer("x", k)))
    for j in range(4):
        conv_core(0, j)
        conv_send(0, j)

    @pl.loop(0, 8)
    def _(i):
        for h in range(2):
            rows = gx[pl.ds(pl.multiple_of(h * 256 + i * 32, 32), 32), :]
            for k in range(2):
                for j in range(4):
                    xo[j, pl.ds(2 * h + k, 32, stride=4), :] = rows[:, k * 512 + j * LANE : k * 512 + (j + 1) * LANE]
        out = jnp.concatenate([xo[j] for j in range(4)], axis=1)
        gfeat_out[pl.ds(pl.multiple_of(i * 128, 128), 128), :] = out.astype(BF)

    await_bytes(frecv.at[low], fg_r.at[2])
    packin[...] = dot(frecv[...].reshape(1024, 512), query[...], TN).astype(BF)
    part = dot(packin[...], gpv[...], NT).astype(BF)
    projp[...] = part.reshape(4, 4, 2, 16, WIDE)
    launch(remote(projp.at[:, :, 1 - c], projr, rs_s.at[2], rs_r.at[4], mate))
    sent(projr, rs_s.at[2])
    await_bytes(nrm1, nm_r.at[1])
    await_bytes(nrm1, nm_s.at[1])
    nrm[...] = nrm[...] + nrm1[0] + nrm1[1] + nrm1[2]
    for n, (i, j) in enumerate(plane):
        launch(remote(nrm, nrm2.at[n], pl_s.at[3], pl_r.at[3], plane_peer("z", "y", i, j)))
    sent(nrm2, pl_s.at[3])
    await_bytes(projr, rs_r.at[4])
    projb[...] = (projp[:, :, c].astype(F32) + projr[...].astype(F32)).astype(BF)
    for n, (i, j) in enumerate(plane):
        launch(
            remote(
                projb.at[(z + i) % 4, (x + j) % 4], proj1.at[n], pl_s.at[4], pl_r.at[4], plane_peer("z", "x", i, j)
            )
        )
    sent(proj1, pl_s.at[4])
    for j in range(4):
        conv_take(1, j)
    for axis in order:
        for j in range(4):
            if conv_axis[0][j] == axis:
                conv_take(0, j)
        conv_last_send(axis)
    packed_out[...] = dot(pall[mine[0], pl.ds(mine[1], 320), :], packin[...]).astype(BF)
    await_bytes(nrm2, pl_r.at[3])
    total = nrm[...]
    for n in range(15):
        total = total + nrm2[n]
    gnorm_out[...] = total
    await_bytes(proj1, pl_r.at[4])
    total = projb[z, x].astype(F32)
    for n in range(15):
        total = total + proj1[n].astype(F32)
    gproj_out[...] = total[:, 0:320]
    for axis in order:
        conv_last_take(axis)

    for ref, sem in sends:
        await_bytes(ref, sem)

    @pl.when(odd == c)
    def _():
        await_bytes(gsendb.at[pl.ds(0, 63)], g_s.at[0])
        await_bytes(gsends, g_s.at[1])

    @pl.when(odd != c)
    def _():
        await_bytes(gsendb, g_s.at[0])
        await_bytes(gsends.at[pl.ds(0, 63)], g_s.at[1])

    await_bytes(fsend.at[pl.ds(0, 31)], a2a_s.at[0])


def finish(
    packed_in, gfeat_in, gconv_in, gproj_in, gnorm_in, packed_out, gfeat_out, gconv_out, gproj_out, gnorm_out, sem
):
    copies = [
        pltpu.make_async_copy(packed_in, packed_out, sem.at[0]),
        pltpu.make_async_copy(gfeat_in, gfeat_out, sem.at[1]),
        pltpu.make_async_copy(gconv_in, gconv_out, sem.at[2]),
        pltpu.make_async_copy(gproj_in, gproj_out, sem.at[3]),
    ]
    for one in (1, 0, 2, 3):
        copies[one].start()
    d = lax.axis_index("dp") * 4 + lax.axis_index("mp")
    for layer in range(2):
        row = gnorm_in[pl.ds(layer * 8 + d // 16, 1), :]
        turned = pltpu.roll(row, LANE - (d % 16) * 8, 1)
        gnorm_out[layer : layer + 1, :] = turned[:, 0:8]
    for one in copies:
        one.wait()


def local(features, lengths, dests, offsets, conv_weight, norm_gain, norm_shift, proj_weight, grad_packed):
    vmem = pl.BlockSpec(memory_space=pltpu.VMEM)
    hbm = pl.BlockSpec(memory_space=pltpu.HBM)
    S = pltpu.SMEM
    V = pltpu.VMEM
    D = pltpu.SemaphoreType.DMA
    scratch = [
        S((32,), jnp.int32), S((32,), jnp.int32), S((32,), jnp.int32), V((2, 512), F32), V((2, 512), F32),
        V((1024, 512), BF), V((2, 1024, 512), BF), V((WIDE, 512), BF), V((WIDE, 512), BF), V((4, 128, LANE), F32),
        V((512, 1024), BF), V((1024, 512), BF), V((256, 256), BF), V((512, 512), F32), V((512, 512), F32), V((512, 512), F32), V((512, LANE), F32),
        V((256, 512), F32), V((256, 512), F32), V((256, LANE), F32),
        V((256, 1024), BF), V((1024, 256), BF), V((256, 512), BF),
        V((4, 4, 8, 1, LANE), F32), V((1024, 512), BF), V((64, 8, 384), BF), V((64, 8, 256), BF), V((2, 32, 8, 384), BF), V((2, 32, 8, 256), BF),
        V((32, 8, 512), BF), V((32, 4, 8, 512), BF), V((2, 640, 512), BF), V((512, 512), BF),
        V((512, 512), F32), V((512, 512), BF), V((512, 1024), F32), V((4, 128, LANE), F32),
        V((2, 4, 4, 4, 2, 4, 8, LANE), BF), V((2, 4, 4, 4, 4, 8, LANE), BF), V((2, 4, 4, 4, 4, 8, LANE), BF),
        V((2, 4, 3, 4, 4, 8, LANE), BF), V((3, 4, 4, 3, 8, LANE), BF), V((3, 15, 3, 8, LANE), BF),
        V((4, 4, 2, 16, WIDE), BF), V((4, 4, 16, WIDE), BF), V((4, 4, 16, WIDE), BF), V((15, 16, WIDE), BF),
        V((16, LANE), F32), V((16, LANE), F32), V((3, 16, LANE), F32), V((15, 16, LANE), F32),
        D((10,)), D((3,)), D((3,)), D((4,)), D((5,)), D((2,)), D((2,)), D((1,)), D((1,)), D((2,)), D((3,)), D((5,)), D((10,)),
        D((2,)), D((2,)), D((5,)), D((5,)),
    ]
    results = ((320, 512), BF), ((1024, 512), BF), ((2, 8, 512), F32), ((16, 320), F32), ((16, LANE), F32)
    middle = pl.pallas_call(
        kernel,
        out_shape=tuple(pltpu.VMEM(*one) for one in results),
        in_specs=[hbm] * 9,
        out_specs=(vmem,) * 5,
        scratch_shapes=scratch,
        compiler_params=pltpu.CompilerParams(collective_id=0, has_side_effects=True, vmem_limit_bytes=65_400_000),
    )(
        lengths, dests, offsets, norm_gain, norm_shift, features.reshape(1024, 512), conv_weight,
        proj_weight.T, grad_packed.T,
    )
    shapes = (*results[:4], ((2, 8), F32))
    packed, gfeat, gconv, gproj, gnorm = pl.pallas_call(
        finish,
        out_shape=tuple(jax.ShapeDtypeStruct(*one) for one in shapes),
        in_specs=[vmem] * 5,
        out_specs=(hbm, hbm, hbm, hbm, vmem),
        scratch_shapes=[D((4,))],
    )(*[pltpu.with_memory_space_constraint(one, pltpu.VMEM) for one in middle])
    return packed.T, gfeat.reshape(32, 32, 512), gconv, gnorm, gproj


def solution(mesh):
    return jax.shard_map(
        local,
        mesh=mesh,
        in_specs=(
            P(("dp", "mp"), None, None),
            P(("dp", "mp")),
            P(("dp", "mp")),
            P(("dp", "mp")),
            P(),
            P(),
            P(),
            P(None, "mp"),
            P("dp", "mp"),
        ),
        out_specs=(
            P("dp", "mp"),
            P(("dp", "mp"), None, None),
            P(None, ("dp", "mp"), None),
            P(None, ("dp", "mp")),
            P("dp", "mp"),
        ),
        check_vma=False,
    )
```

```python
import jax
import jax.numpy as jnp
from jax import lax
from jax.experimental import pallas as pl
from jax.experimental.pallas import tpu as pltpu
from jax.sharding import PartitionSpec as P

EPSILON = 1e-05
BF = jnp.bfloat16
F32 = jnp.float32
MESH = pl.DeviceIdType.MESH
NN = (((1,), (0,)), ((), ()))
NT = (((1,), (1,)), ((), ()))
TN = (((0,), (0,)), ((), ()))
LANE = 128
WIDE = 384


def dot(a, b, dims=NN):
    return lax.dot_general(a, b, dims, preferred_element_type=F32)


def iota(shape, dim):
    return lax.broadcasted_iota(jnp.int32, shape, dim)


def kernel(
    len_hbm, dest_hbm, off_hbm, gain_hbm, shift_hbm, feat_hbm, weight_hbm, proj_hbm, gp_hbm,
    packed_out, gfeat_out, gconv_out, gproj_out, gnorm_out,
    len_ref, dest_ref, off_ref, gain_ref, shift_ref, xb, wv, gpv, gpe, xf, act, actt, placet, pre, xhat0, der0, rstd0, xhat1, der1, rstd1, hid, hidt, frm,
    tbl, query, gsendb, gsends, gbig, gsmall, fsend, frecv, pall, packin,
    gh, gf, gx, xo,
    convp, convr, convb, conv1, convb1, conv2,
    projp, projr, projb, proj1,
    nrm, nrmr, nrm1, nrm2,
    in_sem, idx_s, idx_r, ag_s, ag_r, g_s, g_r, a2a_s, a2a_r, fg_s, fg_r, rs_s, rs_r, nm_s, nm_r, pl_s, pl_r,
):
    dp = lax.axis_index("dp")
    y = lax.axis_index("mp")
    z, q = dp // 8, dp % 8
    x, c = q // 2, q % 2
    odd = y % 2
    mine = (y // 2, pl.multiple_of(odd * 320, 64))

    def dp_of(zz, xx, cc):
        return zz * 8 + xx * 2 + cc

    def remote(src, dst, ssem, rsem, to):
        return pltpu.make_async_remote_copy(
            src_ref=src, dst_ref=dst, send_sem=ssem, recv_sem=rsem, device_id=to, device_id_type=MESH
        )

    def await_bytes(ref, sem):
        pltpu.make_async_copy(ref, ref, sem).wait()

    loads = [
        pltpu.make_async_copy(feat_hbm, xb, in_sem.at[0]),
        pltpu.make_async_copy(weight_hbm, wv, in_sem.at[1]),
        pltpu.make_async_copy(proj_hbm, pall.at[mine[0], pl.ds(mine[1], 320)], in_sem.at[2]),
        pltpu.make_async_copy(gp_hbm, gpv.at[pl.ds(0, 320)], in_sem.at[3]),
        pltpu.make_async_copy(gp_hbm, gpe.at[pl.ds(pl.multiple_of(odd * 64, 64), 320)], in_sem.at[4]),
    ]
    partners = (
        [(dp, (y + k) % 4) for k in range(1, 4)]
        + [(z * 8 + (q + k) % 8, y) for k in range(1, 8)]
        + [(((z + k) % 4) * 8 + q, y) for k in range(1, 4)]
    )
    barrier = pltpu.get_barrier_semaphore()
    for to in partners:
        pl.semaphore_signal(barrier, inc=1, device_id=to, device_id_type=MESH)
    small = [
        pltpu.make_async_copy(source, target, in_sem.at[5 + n])
        for n, (source, target) in enumerate(
            ((len_hbm, len_ref), (dest_hbm, dest_ref), (off_hbm, off_ref), (gain_hbm, gain_ref), (shift_hbm, shift_ref))
        )
    ]
    for one in small:
        one.start()
    for one in (0, 2, 4, 1, 3):
        loads[one].start()
    for one in small:
        one.wait()

    lane = iota((1, LANE), 1)
    row = jnp.full((1, LANE), 64, jnp.int32)
    for p in range(16):
        row = jnp.where(lane == dest_ref[2 * p], off_ref[2 * p] >> 3, row)
    tbl[y, z, q] = row.astype(F32)
    lane = iota((1, 256), 1)
    utterance, step = lane >> 3, lane & 7
    target = jnp.full((1, 256), -1, jnp.int32)
    for u in range(32):
        at = jnp.where(step < len_ref[u], dest_ref[u] * 8 + (off_ref[u] & 7) + step, -1)
        target = jnp.where(utterance == u, at, target)
    place = (iota((256, 256), 0) == target).astype(F32).astype(BF)

    gpv[pl.ds(320, 64), :] = jnp.zeros((64, 512), BF)

    loads[0].wait()

    @pl.loop(0, 8)
    def _(i):
        rows = xb[pl.ds(pl.multiple_of(i * 128, 128), 128), :].astype(F32)
        for j in range(4):
            xf[j] = rows[:, j * LANE : (j + 1) * LANE]
        for k in range(4):
            part = jnp.concatenate([xf[j, pl.ds(k, 32, stride=4), :] for j in range(4)], axis=1)
            act[pl.ds(pl.multiple_of((k // 2) * 256 + i * 32, 32), 32), (k % 2) * 512 : (k % 2) * 512 + 512] = part.astype(BF)

    pl.semaphore_wait(barrier, len(partners))

    sends = []

    def launch(copy):
        copy.start()

    def sent(ref, sem):
        sends.append((ref, sem))

    for k in range(1, 4):
        launch(remote(tbl.at[y, z, q], tbl.at[y, z, q], idx_s.at[0], idx_r.at[0], (((z + k) % 4) * 8 + q, y)))
    loads[2].wait()
    up, down, far = (y + 1) % 4, (y + 3) % 4, (y + 2) % 4

    def shard(yy, start, count):
        at = pl.multiple_of((yy % 2) * 320 + start, 16)
        return pall.at[yy // 2, pl.ds(at, count)]

    own = c * 160
    launch(remote(shard(y, own, 160), shard(y, own, 160), ag_s.at[0], ag_r.at[0], (dp, up)))
    launch(remote(shard(y, own, 160), shard(y, own, 160), ag_s.at[0], ag_r.at[1], (dp, down)))
    sent(pall.at[0, pl.ds(0, 320)], ag_s.at[0])
    loads[4].wait()
    edge = gpe.at[pl.ds(pl.multiple_of(256 - 192 * odd, 64), 64)]
    launch(remote(edge, gpe.at[pl.ds(pl.multiple_of(320 * odd, 64), 64)], ag_s.at[3], ag_r.at[4], (dp, y + 1 - 2 * odd)))
    sent(edge, ag_s.at[3])

    loads[1].wait()
    pre[...] = dot(act[...], wv[0])

    def norm_gelu(source, gain, shift, xhat, der, rstd, start, count):
        v = source[pl.ds(start, count), :]
        mean = jnp.mean(v, axis=-1, keepdims=True)
        centred = v - mean
        spread = jnp.mean(centred * centred, axis=-1, keepdims=True)
        inv = lax.rsqrt(spread + EPSILON)
        normal = centred * inv
        arg = normal * gain + shift
        cdf = 0.5 + 0.5 * lax.erf(arg * (2.0**-0.5))
        xhat[pl.ds(start, count), :] = normal
        der[pl.ds(start, count), :] = cdf + arg * (jnp.exp(-0.5 * arg * arg) * 0.3989422804014327)
        rstd[pl.ds(start, count), :] = jnp.broadcast_to(inv, (count, LANE))
        return arg * cdf

    gain0, shift0 = gain_ref[0:1, :], shift_ref[0:1, :]
    gain1, shift1 = gain_ref[1:2, :], shift_ref[1:2, :]

    def first_rows(lo, hi):
        @pl.loop(lo, hi)
        def _(i):
            start = pl.multiple_of(i * 32, 32)
            for h in range(2):
                out = norm_gelu(pre, gain0, shift0, xhat0, der0, rstd0, pl.multiple_of(start + h * 256, 32), 32)
                hid[pl.ds(start, 32), h * 512 : (h + 1) * 512] = out.astype(BF)

    first_rows(0, 4)
    await_bytes(tbl.at[y, pl.ds(0, 3), 0], idx_r.at[0])
    sent(tbl.at[y, pl.ds(0, 3), 0], idx_s.at[0])
    for k in range(1, 8):
        launch(remote(tbl.at[y, :, q], tbl.at[y, :, q], idx_s.at[1], idx_r.at[1], (z * 8 + (q + k) % 8, y)))

    first_rows(4, 8)
    pre[pl.ds(0, 256), :] = dot(hid[...], wv[1])

    @pl.loop(0, 4)
    def _(i):
        for h in range(2):
            start = pl.multiple_of(i * 64 + h * 32, 32)
            out = norm_gelu(pre, gain1, shift1, xhat1, der1, rstd1, start, 32)
            frm[pl.ds(start, 32), :] = out.astype(BF)

    fsend[...] = dot(place, frm[...]).astype(BF).reshape(32, 8, 512)

    await_bytes(tbl.at[y, :, pl.ds(0, 7)], idx_r.at[1])
    sent(tbl.at[y, :, pl.ds(0, 7)], idx_s.at[1])
    for k in range(1, 4):
        launch(remote(tbl.at[y], tbl.at[y], idx_s.at[2], idx_r.at[2], (dp, (y + k) % 4)))
    own_f = pltpu.make_async_copy(fsend.at[dp], frecv.at[dp, y], a2a_r.at[0])
    own_f.start()

    @pl.loop(1, 32)
    def _(k):
        to = (dp + k) % 32
        remote(fsend.at[to], frecv.at[dp, y], a2a_s.at[0], a2a_r.at[0], (to, y)).start()

    await_bytes(shard(down, own, 160), ag_r.at[0])
    launch(remote(shard(down, own, 80), shard(down, own, 80), ag_s.at[1], ag_r.at[2], (dp, up)))
    await_bytes(shard(up, own, 160), ag_r.at[1])
    launch(remote(shard(up, own + 80, 80), shard(up, own + 80, 80), ag_s.at[1], ag_r.at[2], (dp, down)))
    sent(shard(y, 0, 160), ag_s.at[1])

    loads[3].wait()
    await_bytes(gpe.at[pl.ds(0, 64)], ag_r.at[4])
    pick = (iota((128, 512), 0) == dp).astype(F32).astype(BF)
    column = (iota((128, 512), 1) - (iota((128, 512), 0) & 7)).astype(F32)
    slot = iota((128, 128), 0) >> 3
    wanted = (slot & 3) * 32 + (slot >> 2) * 2
    await_bytes(tbl.at[pl.ds(0, 3)], idx_r.at[2])
    sent(tbl.at[pl.ds(0, 3)], idx_s.at[2])
    table = jnp.concatenate([tbl[m].reshape(32, LANE) for m in range(4)], axis=0).astype(BF)
    blocks = dot(table, pick).astype(BF)

    for turn in (2, 1, 3, 0):
        part = (z + turn) % 4
        for kind, (source, landing) in enumerate(((gsendb, gbig), (gsends, gsmall))):
            core = odd if kind == 0 else 1 - odd
            spread = (wanted + part * 8 + core == iota((128, 128), 1)).astype(F32).astype(BF)
            one_hot = (dot(spread, blocks) * 8.0 == column).astype(F32).astype(BF)
            if kind == 0:
                values = dot(one_hot, gpe[...], NT)
                gsendb[pl.ds(part * 16, 16)] = values.astype(BF).reshape(16, 8, 384)
            else:
                values = dot(one_hot, gpe[pl.ds(pl.multiple_of(128 * odd, 128), 256), :], NT)
                gsends[pl.ds(part * 16, 16)] = values.astype(BF).reshape(16, 8, 256)
            for along in (2, 1, 3, 0):
                for across in (2, 1, 3, 0):
                    side = (y + across) % 4
                    column_x = (x + along) % 4
                    src = source.at[part * 16 + column_x * 4 + side]
                    dst = landing.at[y // 2, dp]
                    copy = remote(src, dst, g_s.at[kind], g_r.at[kind], (dp_of(part, column_x, core), side))
                    if turn or along or across:
                        copy.start()
                    else:
                        pl.when(core != c)(copy.start)
                        pl.when(core == c)(pltpu.make_async_copy(src, dst, g_r.at[kind]).start)

    await_bytes(shard(far, own, 160), ag_r.at[2])
    mate = (dp_of(z, x, 1 - c), y)
    for at in (up, down, far):
        launch(remote(shard(at, own, 160), shard(at, own, 160), ag_s.at[2], ag_r.at[3], mate))
    sent(pall.at[0, pl.ds(0, 480)], ag_s.at[2])

    placet[...] = place.T
    for part in range(4):
        slot = (iota((256, 128), 0) >> 3) + part * 32
        spread = ((slot & 3) * 32 + (slot >> 2) == iota((256, 128), 1)).astype(F32).astype(BF)
        column = (iota((256, 512), 1) - (iota((256, 512), 0) & 7)).astype(F32)
        query[part * 256 : part * 256 + 256, :] = (dot(spread, blocks) * 8.0 == column).astype(F32).astype(BF)
    actt[...] = act[...].T
    hidt[...] = hid[...].T
    await_bytes(pall.at[0, pl.ds(0, 480)], ag_r.at[3])
    await_bytes(frecv.at[:, 0], a2a_r.at[0])
    low, high = pl.ds(0, 16), pl.ds(16, 16)
    for n, (to, half) in enumerate(((up, low), (down, high), (up, high), (down, low))):
        launch(remote(frecv.at[half, y], frecv.at[half, y], fg_s.at[0], fg_r.at[min(n, 2)], (dp, to)))
    sent(frecv.at[low], fg_s.at[0])
    await_bytes(gbig, g_r.at[0])
    await_bytes(gsmall, g_r.at[1])

    total = None
    for m in range(2):
        part = dot(gbig[m].reshape(256, 384), pall[m, pl.ds(pl.multiple_of(256 * c, 128), 384), :])
        total = part if total is None else total + part
        total = total + dot(gsmall[m].reshape(256, 256), pall[m, pl.ds(pl.multiple_of(384 - 384 * c, 128), 256), :])
    grad_frames = dot(placet[...], total.astype(BF))
    gh[pl.ds(0, 256), :] = grad_frames

    sizes = dict(x=x, y=y, z=z)

    def peer(axis, k):
        if axis == "x":
            return (dp_of(z, (x + k) % 4, c), y)
        if axis == "z":
            return (dp_of((z + k) % 4, x, c), y)
        return (dp, (y + k) % 4)

    def chunk(ref, lead, dims, axis, at):
        pos = dims.index(axis)
        return ref.at[tuple(lead) + (slice(None),) * pos + (at,)]

    def scatter(source, landing, lead, dims, axis, send, sem):
        for k in range(1, 4):
            at = (sizes[axis] + k) % 4
            launch(
                remote(
                    chunk(source, lead, dims, axis, at),
                    landing.at[tuple(lead) + (k - 1,)],
                    rs_s.at[send],
                    rs_r.at[sem],
                    peer(axis, k),
                )
            )

    def gather(source, landing, lead, dims, axis):
        total = chunk(source, lead, dims, axis, sizes[axis])[...].astype(F32)
        for k in range(3):
            total = total + landing[tuple(lead) + (k,)].astype(F32)
        return total

    def norm_back(upstream, gain, xhat, der, rstd, start, count, sums):
        dy = upstream * der[pl.ds(start, count), :]
        normal = xhat[pl.ds(start, count), :]
        dyn = dy * normal
        dg = sums[0] + dyn.reshape(count // 8, 8, 512).sum(axis=0)
        ds = sums[1] + dy.reshape(count // 8, 8, 512).sum(axis=0)
        mean_d = jnp.mean(dy * gain, axis=-1, keepdims=True)
        mean_dn = jnp.mean(dyn * gain, axis=-1, keepdims=True)
        inv = rstd[pl.ds(start, count), :][:, 0:1]
        return inv * (dy * gain - mean_d - normal * mean_dn), (dg, ds)

    def put_norm(layer, sums):
        for half in range(2):
            row = sums[half].sum(axis=0, keepdims=True)
            for j in range(4):
                nrm[layer * 8 + half * 4 + j : layer * 8 + half * 4 + j + 1, :] = row[:, j * LANE : (j + 1) * LANE]

    zeros = (jnp.zeros((8, 512), F32), jnp.zeros((8, 512), F32))

    def second_body(i, sums):
        for h in range(2):
            start = pl.multiple_of(i * 64 + h * 32, 32)
            out, sums = norm_back(gh[pl.ds(start, 32), :], gain1, xhat1, der1, rstd1, start, 32, sums)
            gf[pl.ds(start, 32), :] = out.astype(BF)
        return sums

    sums1 = lax.fori_loop(0, 4, second_body, zeros)
    put_norm(1, sums1)
    grad_second = gf[pl.ds(0, 256), :]
    for h in range(2):
        gh[pl.ds(h * 256, 256), :] = dot(grad_second, wv[1, pl.ds(h * 512, 512), :], NT).astype(BF).astype(F32)

    def forward_frames():
        await_bytes(frecv.at[low, down], fg_r.at[0])
        launch(remote(frecv.at[low, down], frecv.at[low, down], fg_s.at[1], fg_r.at[2], (dp, up)))
        await_bytes(frecv.at[high, up], fg_r.at[1])
        launch(remote(frecv.at[high, up], frecv.at[high, up], fg_s.at[1], fg_r.at[2], (dp, down)))
        sent(frecv.at[:, y], fg_s.at[1])

    def kernel_grad(layer, left):
        for half in range(2):
            right = gf[0 : left.shape[1], half * 256 : half * 256 + 256]
            for h in range(4):
                part = dot(left[h * 256 : (h + 1) * 256, :], right).astype(BF)
                for j in range(2):
                    convp[layer, 2 * half + j, h] = part[:, j * LANE : (j + 1) * LANE].reshape(4, 2, 4, 8, LANE)
            for j in (2 * half, 2 * half + 1):
                launch(remote(convp.at[layer, j, :, :, 1 - c], convr.at[layer, j], rs_s.at[layer], rs_r.at[2 * layer + half], mate))
        sent(convr.at[layer], rs_s.at[layer])

    kernel_grad(1, hidt)
    forward_frames()

    def conv_core(layer, j):
        if j % 2 == 0:
            await_bytes(convr.at[layer, pl.ds(j, 2)], rs_r.at[2 * layer + j // 2])
        convb[layer, j] = (
            convp[layer, j, :, :, c].astype(F32) + convr[layer, j].astype(F32)
        ).astype(BF)

    base = ("z", "x", "y")
    plane = sorted([(i, j) for i in range(4) for j in range(4) if i or j], key=lambda one: one.count(2) * 5 + 4 - one.count(0), reverse=True)

    conv_axis = (("x", "z", "y", "y"), ("x", "z", "x", "z"))
    groups = {
        axis: [(layer, j) for layer in range(2) for j in range(4) if conv_axis[layer][j] == axis] for axis in "xyz"
    }
    order = "xyz"

    def others_of(axis):
        return tuple(one for one in base if one != axis)

    def conv_send(layer, j):
        scatter(convb, conv1, (layer, j), base, conv_axis[layer][j], 3 + layer, 5 if layer else 6 + j)
        if j == 3:
            sent(conv1.at[layer], rs_s.at[3 + layer])

    def conv_take(layer, j):
        axis = conv_axis[layer][j]
        if layer == 0:
            await_bytes(conv1.at[layer, j], rs_r.at[6 + j])
        elif j == 0:
            await_bytes(conv1.at[layer], rs_r.at[5])
        total = gather(convb, conv1, (layer, j), base, axis)
        convb1[order.index(axis), :, :, groups[axis].index((layer, j))] = total.astype(BF)

    def plane_peer(first, second, i, j):
        at = dict(sizes)
        at[first] = (at[first] + i) % 4
        at[second] = (at[second] + j) % 4
        return (dp_of(at["z"], at["x"], c), at["y"])

    def conv_last_send(axis):
        p, count = order.index(axis), len(groups[axis])
        first, second = others_of(axis)
        for n, (i, j) in enumerate(plane):
            launch(
                remote(
                    convb1.at[p, (sizes[first] + i) % 4, (sizes[second] + j) % 4, pl.ds(0, count)],
                    conv2.at[p, n, pl.ds(0, count)],
                    pl_s.at[p],
                    pl_r.at[p],
                    plane_peer(first, second, i, j),
                )
            )
        sent(conv2.at[p, :, pl.ds(0, count)], pl_s.at[p])

    def conv_last_take(axis):
        p, count = order.index(axis), len(groups[axis])
        first, second = others_of(axis)
        await_bytes(conv2.at[p, :, pl.ds(0, count)], pl_r.at[p])
        total = convb1[p, sizes[first], sizes[second], 0:count].astype(F32)
        for n in range(15):
            total = total + conv2[p, n, 0:count].astype(F32)
        for at, (layer, j) in enumerate(groups[axis]):
            gconv_out[layer, :, j * LANE : (j + 1) * LANE] = total[at]

    def first_body(i, sums):
        for h in range(2):
            start = pl.multiple_of(i * 64 + h * 32, 32)
            out, sums = norm_back(gh[pl.ds(start, 32), :], gain0, xhat0, der0, rstd0, start, 32, sums)
            gf[pl.ds(start, 32), :] = out.astype(BF)
        return sums

    sums0 = lax.fori_loop(0, 8, first_body, zeros)
    put_norm(0, sums0)
    to_mate = remote(nrm, nrmr, nm_s.at[0], nm_r.at[0], mate)
    to_mate.start()

    for j in range(4):
        conv_core(1, j)
        conv_send(1, j)
    kernel_grad(0, actt)
    for h in range(2):
        gx[pl.ds(h * 256, 256), :] = dot(gf[pl.ds(h * 256, 256), :], wv[0], NT)
    await_bytes(nrmr, nm_r.at[0])
    to_mate.wait_send()
    nrm[...] = nrm[...] + nrmr[...]
    for k in range(1, 4):
        launch(remote(nrm, nrm1.at[k - 1], nm_s.at[1], nm_r.at[1], peer("x", k)))
    for j in range(4):
        conv_core(0, j)
        conv_send(0, j)

    @pl.loop(0, 8)
    def _(i):
        for h in range(2):
            rows = gx[pl.ds(pl.multiple_of(h * 256 + i * 32, 32), 32), :]
            for k in range(2):
                for j in range(4):
                    xo[j, pl.ds(2 * h + k, 32, stride=4), :] = rows[:, k * 512 + j * LANE : k * 512 + (j + 1) * LANE]
        out = jnp.concatenate([xo[j] for j in range(4)], axis=1)
        gfeat_out[pl.ds(pl.multiple_of(i * 128, 128), 128), :] = out.astype(BF)

    await_bytes(frecv.at[low], fg_r.at[2])
    packin[...] = dot(frecv[...].reshape(1024, 512), query[...], TN).astype(BF)
    part = dot(packin[...], gpv[...], NT).astype(BF)
    projp[...] = part.reshape(4, 4, 2, 16, WIDE)
    launch(remote(projp.at[:, :, 1 - c], projr, rs_s.at[2], rs_r.at[4], mate))
    sent(projr, rs_s.at[2])
    packed_out[...] = dot(pall[mine[0], pl.ds(mine[1], 320), :], packin[...]).astype(BF)
    await_bytes(projr, rs_r.at[4])
    projb[...] = (projp[:, :, c].astype(F32) + projr[...].astype(F32)).astype(BF)
    for n, (i, j) in enumerate(plane):
        launch(
            remote(
                projb.at[(z + i) % 4, (x + j) % 4], proj1.at[n], pl_s.at[4], pl_r.at[4], plane_peer("z", "x", i, j)
            )
        )
    sent(proj1, pl_s.at[4])
    await_bytes(nrm1, nm_r.at[1])
    await_bytes(nrm1, nm_s.at[1])
    nrm[...] = nrm[...] + nrm1[0] + nrm1[1] + nrm1[2]
    for n, (i, j) in enumerate(plane):
        launch(remote(nrm, nrm2.at[n], pl_s.at[3], pl_r.at[3], plane_peer("z", "y", i, j)))
    sent(nrm2, pl_s.at[3])
    for j in range(4):
        conv_take(1, j)
    for axis in "xzy":
        for j in range(4):
            if conv_axis[0][j] == axis:
                conv_take(0, j)
        conv_last_send(axis)
    await_bytes(nrm2, pl_r.at[3])
    total = nrm[...]
    for n in range(15):
        total = total + nrm2[n]
    gnorm_out[...] = total
    await_bytes(proj1, pl_r.at[4])
    total = projb[z, x].astype(F32)
    for n in range(15):
        total = total + proj1[n].astype(F32)
    gproj_out[...] = total[:, 0:320]
    for axis in "xzy":
        conv_last_take(axis)

    for ref, sem in sends:
        await_bytes(ref, sem)

    @pl.when(odd == c)
    def _():
        await_bytes(gsendb.at[pl.ds(0, 63)], g_s.at[0])
        await_bytes(gsends, g_s.at[1])

    @pl.when(odd != c)
    def _():
        await_bytes(gsendb, g_s.at[0])
        await_bytes(gsends.at[pl.ds(0, 63)], g_s.at[1])

    await_bytes(fsend.at[pl.ds(0, 31)], a2a_s.at[0])


def finish(
    packed_in, gfeat_in, gconv_in, gproj_in, gnorm_in, packed_out, gfeat_out, gconv_out, gproj_out, gnorm_out, rows, sem
):
    copies = [
        pltpu.make_async_copy(packed_in, packed_out, sem.at[0]),
        pltpu.make_async_copy(gfeat_in, gfeat_out, sem.at[1]),
        pltpu.make_async_copy(gconv_in, gconv_out, sem.at[2]),
        pltpu.make_async_copy(gproj_in, gproj_out, sem.at[3]),
    ]
    for one in (1, 0, 2, 3):
        copies[one].start()
    d = lax.axis_index("dp") * 4 + lax.axis_index("mp")
    for layer in range(2):
        row = gnorm_in[pl.ds(layer * 8 + d // 16, 1), :]
        turned = pltpu.roll(row, LANE - (d % 16) * 8, 1)
        rows[layer : layer + 1, :] = turned[:, 0:8]
    copies.append(pltpu.make_async_copy(rows, gnorm_out, sem.at[4]))
    copies[-1].start()
    for one in copies:
        one.wait()


def local(features, lengths, dests, offsets, conv_weight, norm_gain, norm_shift, proj_weight, grad_packed):
    vmem = pl.BlockSpec(memory_space=pltpu.VMEM)
    hbm = pl.BlockSpec(memory_space=pltpu.HBM)
    S = pltpu.SMEM
    V = pltpu.VMEM
    D = pltpu.SemaphoreType.DMA
    scratch = [
        S((32,), jnp.int32), S((32,), jnp.int32), S((32,), jnp.int32), V((2, 512), F32), V((2, 512), F32),
        V((1024, 512), BF), V((2, 1024, 512), BF), V((WIDE, 512), BF), V((WIDE, 512), BF), V((4, 128, LANE), F32),
        V((512, 1024), BF), V((1024, 512), BF), V((256, 256), BF), V((512, 512), F32), V((512, 512), F32), V((512, 512), F32), V((512, LANE), F32),
        V((256, 512), F32), V((256, 512), F32), V((256, LANE), F32),
        V((256, 1024), BF), V((1024, 256), BF), V((256, 512), BF),
        V((4, 4, 8, 1, LANE), F32), V((1024, 512), BF), V((64, 8, 384), BF), V((64, 8, 256), BF), V((2, 32, 8, 384), BF), V((2, 32, 8, 256), BF),
        V((32, 8, 512), BF), V((32, 4, 8, 512), BF), V((2, 640, 512), BF), V((512, 512), BF),
        V((512, 512), F32), V((512, 512), BF), V((512, 1024), F32), V((4, 128, LANE), F32),
        V((2, 4, 4, 4, 2, 4, 8, LANE), BF), V((2, 4, 4, 4, 4, 8, LANE), BF), V((2, 4, 4, 4, 4, 8, LANE), BF),
        V((2, 4, 3, 4, 4, 8, LANE), BF), V((3, 4, 4, 3, 8, LANE), BF), V((3, 15, 3, 8, LANE), BF),
        V((4, 4, 2, 16, WIDE), BF), V((4, 4, 16, WIDE), BF), V((4, 4, 16, WIDE), BF), V((15, 16, WIDE), BF),
        V((16, LANE), F32), V((16, LANE), F32), V((3, 16, LANE), F32), V((15, 16, LANE), F32),
        D((10,)), D((3,)), D((3,)), D((4,)), D((5,)), D((2,)), D((2,)), D((1,)), D((1,)), D((2,)), D((3,)), D((5,)), D((10,)),
        D((2,)), D((2,)), D((5,)), D((5,)),
    ]
    results = ((320, 512), BF), ((1024, 512), BF), ((2, 8, 512), F32), ((16, 320), F32), ((16, LANE), F32)
    middle = pl.pallas_call(
        kernel,
        out_shape=tuple(pltpu.VMEM(*one) for one in results),
        in_specs=[hbm] * 9,
        out_specs=(vmem,) * 5,
        scratch_shapes=scratch,
        compiler_params=pltpu.CompilerParams(collective_id=0, has_side_effects=True, vmem_limit_bytes=65_400_000),
    )(
        lengths, dests, offsets, norm_gain, norm_shift, features.reshape(1024, 512), conv_weight,
        proj_weight.T, grad_packed.T,
    )
    shapes = (*results[:4], ((2, 8), F32))
    packed, gfeat, gconv, gproj, gnorm = pl.pallas_call(
        finish,
        out_shape=tuple(jax.ShapeDtypeStruct(*one) for one in shapes),
        in_specs=[vmem] * 5,
        out_specs=(hbm,) * 5,
        scratch_shapes=[V((2, 8), F32), D((5,))],
    )(*[pltpu.with_memory_space_constraint(one, pltpu.VMEM) for one in middle])
    return packed.T, gfeat.reshape(32, 32, 512), gconv, gnorm, gproj


def solution(mesh):
    return jax.shard_map(
        local,
        mesh=mesh,
        in_specs=(
            P(("dp", "mp"), None, None),
            P(("dp", "mp")),
            P(("dp", "mp")),
            P(("dp", "mp")),
            P(),
            P(),
            P(),
            P(None, "mp"),
            P("dp", "mp"),
        ),
        out_specs=(
            P("dp", "mp"),
            P(("dp", "mp"), None, None),
            P(None, ("dp", "mp"), None),
            P(None, ("dp", "mp")),
            P("dp", "mp"),
        ),
        check_vma=False,
    )
```

```python
import jax
import jax.numpy as jnp
from jax import lax
from jax.experimental import pallas as pl
from jax.experimental.pallas import tpu as pltpu
from jax.sharding import PartitionSpec as P

EPSILON = 1e-05
BF = jnp.bfloat16
F32 = jnp.float32
MESH = pl.DeviceIdType.MESH
NN = (((1,), (0,)), ((), ()))
NT = (((1,), (1,)), ((), ()))
TN = (((0,), (0,)), ((), ()))
LANE = 128
WIDE = 384


def dot(a, b, dims=NN):
    return lax.dot_general(a, b, dims, preferred_element_type=F32)


def iota(shape, dim):
    return lax.broadcasted_iota(jnp.int32, shape, dim)


def kernel(
    len_hbm, dest_hbm, off_hbm, gain_hbm, shift_hbm, feat_hbm, weight_hbm, proj_hbm, gp_hbm,
    packed_out, gfeat_out, gconv_out, gproj_out, gnorm_out,
    len_ref, dest_ref, off_ref, gain_ref, shift_ref, xb, wv, gpv, gpe, xf, act, actt, placet, pre, xhat0, der0, rstd0, xhat1, der1, rstd1, hid, hidt, frm,
    tbl, query, gsendb, gsends, gbig, gsmall, fsend, frecv, pall, packin,
    gh, gf, gx, xo,
    convp, convr, convb, conv1, convb1, conv2,
    projp, projr, projb, proj1,
    nrm, nrmr, nrm1, nrm2,
    in_sem, idx_s, idx_r, ag_s, ag_r, g_s, g_r, a2a_s, a2a_r, fg_s, fg_r, rs_s, rs_r, nm_s, nm_r, pl_s, pl_r,
):
    dp = lax.axis_index("dp")
    y = lax.axis_index("mp")
    z, q = dp // 8, dp % 8
    x, c = q // 2, q % 2
    odd = y % 2
    mine = (y // 2, pl.multiple_of(odd * 320, 64))

    def dp_of(zz, xx, cc):
        return zz * 8 + xx * 2 + cc

    def remote(src, dst, ssem, rsem, to):
        return pltpu.make_async_remote_copy(
            src_ref=src, dst_ref=dst, send_sem=ssem, recv_sem=rsem, device_id=to, device_id_type=MESH
        )

    def await_bytes(ref, sem):
        pltpu.make_async_copy(ref, ref, sem).wait()

    loads = [
        pltpu.make_async_copy(feat_hbm, xb, in_sem.at[0]),
        pltpu.make_async_copy(weight_hbm, wv, in_sem.at[1]),
        pltpu.make_async_copy(proj_hbm, pall.at[mine[0], pl.ds(mine[1], 320)], in_sem.at[2]),
        pltpu.make_async_copy(gp_hbm, gpv.at[pl.ds(0, 320)], in_sem.at[3]),
        pltpu.make_async_copy(gp_hbm, gpe.at[pl.ds(pl.multiple_of(odd * 64, 64), 320)], in_sem.at[4]),
    ]
    partners = (
        [(dp, (y + k) % 4) for k in range(1, 4)]
        + [(z * 8 + (q + k) % 8, y) for k in range(1, 8)]
        + [(((z + k) % 4) * 8 + q, y) for k in range(1, 4)]
    )
    barrier = pltpu.get_barrier_semaphore()
    for to in partners:
        pl.semaphore_signal(barrier, inc=1, device_id=to, device_id_type=MESH)
    small = [
        pltpu.make_async_copy(source, target, in_sem.at[5 + n])
        for n, (source, target) in enumerate(
            ((len_hbm, len_ref), (dest_hbm, dest_ref), (off_hbm, off_ref), (gain_hbm, gain_ref), (shift_hbm, shift_ref))
        )
    ]
    for one in small:
        one.start()
    for one in (0, 2, 4, 1, 3):
        loads[one].start()
    for one in small:
        one.wait()

    lane = iota((1, LANE), 1)
    row = jnp.full((1, LANE), 64, jnp.int32)
    for p in range(16):
        row = jnp.where(lane == dest_ref[2 * p], off_ref[2 * p] >> 3, row)
    tbl[y, z, q] = row.astype(F32)
    lane = iota((1, 256), 1)
    utterance, step = lane >> 3, lane & 7
    target = jnp.full((1, 256), -1, jnp.int32)
    for u in range(32):
        at = jnp.where(step < len_ref[u], dest_ref[u] * 8 + (off_ref[u] & 7) + step, -1)
        target = jnp.where(utterance == u, at, target)
    place = (iota((256, 256), 0) == target).astype(F32).astype(BF)

    gpv[pl.ds(320, 64), :] = jnp.zeros((64, 512), BF)

    loads[0].wait()

    @pl.loop(0, 8)
    def _(i):
        rows = xb[pl.ds(pl.multiple_of(i * 128, 128), 128), :].astype(F32)
        for j in range(4):
            xf[j] = rows[:, j * LANE : (j + 1) * LANE]
        for k in range(4):
            part = jnp.concatenate([xf[j, pl.ds(k, 32, stride=4), :] for j in range(4)], axis=1)
            act[pl.ds(pl.multiple_of((k // 2) * 256 + i * 32, 32), 32), (k % 2) * 512 : (k % 2) * 512 + 512] = part.astype(BF)

    pl.semaphore_wait(barrier, len(partners))

    sends = []

    def launch(copy):
        copy.start()

    def sent(ref, sem):
        sends.append((ref, sem))

    for k in range(1, 4):
        launch(remote(tbl.at[y, z, q], tbl.at[y, z, q], idx_s.at[0], idx_r.at[0], (((z + k) % 4) * 8 + q, y)))
    loads[2].wait()
    up, down, far = (y + 1) % 4, (y + 3) % 4, (y + 2) % 4

    def shard(yy, start, count):
        at = pl.multiple_of((yy % 2) * 320 + start, 16)
        return pall.at[yy // 2, pl.ds(at, count)]

    own = c * 160
    launch(remote(shard(y, own, 160), shard(y, own, 160), ag_s.at[0], ag_r.at[0], (dp, up)))
    launch(remote(shard(y, own, 160), shard(y, own, 160), ag_s.at[0], ag_r.at[1], (dp, down)))
    sent(pall.at[0, pl.ds(0, 320)], ag_s.at[0])
    loads[4].wait()
    edge = gpe.at[pl.ds(pl.multiple_of(256 - 192 * odd, 64), 64)]
    launch(remote(edge, gpe.at[pl.ds(pl.multiple_of(320 * odd, 64), 64)], ag_s.at[3], ag_r.at[4], (dp, y + 1 - 2 * odd)))
    sent(edge, ag_s.at[3])

    loads[1].wait()
    pre[...] = dot(act[...], wv[0])

    def norm_gelu(source, gain, shift, xhat, der, rstd, start, count):
        v = source[pl.ds(start, count), :]
        mean = jnp.mean(v, axis=-1, keepdims=True)
        centred = v - mean
        spread = jnp.mean(centred * centred, axis=-1, keepdims=True)
        inv = lax.rsqrt(spread + EPSILON)
        normal = centred * inv
        arg = normal * gain + shift
        cdf = 0.5 + 0.5 * lax.erf(arg * (2.0**-0.5))
        xhat[pl.ds(start, count), :] = normal
        der[pl.ds(start, count), :] = cdf + arg * (jnp.exp(-0.5 * arg * arg) * 0.3989422804014327)
        rstd[pl.ds(start, count), :] = jnp.broadcast_to(inv, (count, LANE))
        return arg * cdf

    gain0, shift0 = gain_ref[0:1, :], shift_ref[0:1, :]
    gain1, shift1 = gain_ref[1:2, :], shift_ref[1:2, :]

    def first_rows(lo, hi):
        @pl.loop(lo, hi)
        def _(i):
            start = pl.multiple_of(i * 32, 32)
            for h in range(2):
                out = norm_gelu(pre, gain0, shift0, xhat0, der0, rstd0, pl.multiple_of(start + h * 256, 32), 32)
                hid[pl.ds(start, 32), h * 512 : (h + 1) * 512] = out.astype(BF)

    first_rows(0, 4)
    await_bytes(tbl.at[y, pl.ds(0, 3), 0], idx_r.at[0])
    sent(tbl.at[y, pl.ds(0, 3), 0], idx_s.at[0])
    for k in range(1, 8):
        launch(remote(tbl.at[y, :, q], tbl.at[y, :, q], idx_s.at[1], idx_r.at[1], (z * 8 + (q + k) % 8, y)))

    first_rows(4, 8)
    pre[pl.ds(0, 256), :] = dot(hid[...], wv[1])

    @pl.loop(0, 4)
    def _(i):
        for h in range(2):
            start = pl.multiple_of(i * 64 + h * 32, 32)
            out = norm_gelu(pre, gain1, shift1, xhat1, der1, rstd1, start, 32)
            frm[pl.ds(start, 32), :] = out.astype(BF)

    fsend[...] = dot(place, frm[...]).astype(BF).reshape(32, 8, 512)

    await_bytes(tbl.at[y, :, pl.ds(0, 7)], idx_r.at[1])
    sent(tbl.at[y, :, pl.ds(0, 7)], idx_s.at[1])
    for k in range(1, 4):
        launch(remote(tbl.at[y], tbl.at[y], idx_s.at[2], idx_r.at[2], (dp, (y + k) % 4)))
    own_f = pltpu.make_async_copy(fsend.at[dp], frecv.at[dp, y], a2a_r.at[0])
    own_f.start()

    @pl.loop(1, 32)
    def _(k):
        to = (dp + k) % 32
        remote(fsend.at[to], frecv.at[dp, y], a2a_s.at[0], a2a_r.at[0], (to, y)).start()

    await_bytes(shard(down, own, 160), ag_r.at[0])
    launch(remote(shard(down, own, 80), shard(down, own, 80), ag_s.at[1], ag_r.at[2], (dp, up)))
    await_bytes(shard(up, own, 160), ag_r.at[1])
    launch(remote(shard(up, own + 80, 80), shard(up, own + 80, 80), ag_s.at[1], ag_r.at[2], (dp, down)))
    sent(shard(y, 0, 160), ag_s.at[1])

    loads[3].wait()
    await_bytes(gpe.at[pl.ds(0, 64)], ag_r.at[4])
    pick = (iota((128, 512), 0) == dp).astype(F32).astype(BF)
    column = (iota((128, 512), 1) - (iota((128, 512), 0) & 7)).astype(F32)
    slot = iota((128, 128), 0) >> 3
    wanted = (slot & 3) * 32 + (slot >> 2) * 2
    await_bytes(tbl.at[pl.ds(0, 3)], idx_r.at[2])
    sent(tbl.at[pl.ds(0, 3)], idx_s.at[2])
    table = jnp.concatenate([tbl[m].reshape(32, LANE) for m in range(4)], axis=0).astype(BF)
    blocks = dot(table, pick).astype(BF)

    for turn in (2, 1, 3, 0):
        part = (z + turn) % 4
        for kind, (source, landing) in enumerate(((gsendb, gbig), (gsends, gsmall))):
            core = odd if kind == 0 else 1 - odd
            spread = (wanted + part * 8 + core == iota((128, 128), 1)).astype(F32).astype(BF)
            one_hot = (dot(spread, blocks) * 8.0 == column).astype(F32).astype(BF)
            if kind == 0:
                values = dot(one_hot, gpe[...], NT)
                gsendb[pl.ds(part * 16, 16)] = values.astype(BF).reshape(16, 8, 384)
            else:
                values = dot(one_hot, gpe[pl.ds(pl.multiple_of(128 * odd, 128), 256), :], NT)
                gsends[pl.ds(part * 16, 16)] = values.astype(BF).reshape(16, 8, 256)
            for along in (2, 1, 3, 0):
                for across in (2, 1, 3, 0):
                    side = (y + across) % 4
                    column_x = (x + along) % 4
                    src = source.at[part * 16 + column_x * 4 + side]
                    dst = landing.at[y // 2, dp]
                    copy = remote(src, dst, g_s.at[kind], g_r.at[kind], (dp_of(part, column_x, core), side))
                    if turn or along or across:
                        copy.start()
                    else:
                        pl.when(core != c)(copy.start)
                        pl.when(core == c)(pltpu.make_async_copy(src, dst, g_r.at[kind]).start)

    await_bytes(shard(far, own, 160), ag_r.at[2])
    mate = (dp_of(z, x, 1 - c), y)
    for at in (up, down, far):
        launch(remote(shard(at, own, 160), shard(at, own, 160), ag_s.at[2], ag_r.at[3], mate))
    sent(pall.at[0, pl.ds(0, 480)], ag_s.at[2])

    await_bytes(frecv.at[:, 0], a2a_r.at[0])
    low, high = pl.ds(0, 16), pl.ds(16, 16)
    for n, (to, half) in enumerate(((up, low), (down, high), (up, high), (down, low))):
        launch(remote(frecv.at[half, y], frecv.at[half, y], fg_s.at[0], fg_r.at[min(n, 2)], (dp, to)))
    sent(frecv.at[low], fg_s.at[0])
    placet[...] = place.T
    for part in range(4):
        slot = (iota((256, 128), 0) >> 3) + part * 32
        spread = ((slot & 3) * 32 + (slot >> 2) == iota((256, 128), 1)).astype(F32).astype(BF)
        column = (iota((256, 512), 1) - (iota((256, 512), 0) & 7)).astype(F32)
        query[part * 256 : part * 256 + 256, :] = (dot(spread, blocks) * 8.0 == column).astype(F32).astype(BF)
    actt[...] = act[...].T
    hidt[...] = hid[...].T
    await_bytes(gbig, g_r.at[0])
    await_bytes(gsmall, g_r.at[1])
    await_bytes(pall.at[0, pl.ds(0, 480)], ag_r.at[3])

    total = None
    for m in range(2):
        part = dot(gbig[m].reshape(256, 384), pall[m, pl.ds(pl.multiple_of(256 * c, 128), 384), :])
        total = part if total is None else total + part
        total = total + dot(gsmall[m].reshape(256, 256), pall[m, pl.ds(pl.multiple_of(384 - 384 * c, 128), 256), :])
    grad_frames = dot(placet[...], total.astype(BF))
    gh[pl.ds(0, 256), :] = grad_frames

    sizes = dict(x=x, y=y, z=z)

    def peer(axis, k):
        if axis == "x":
            return (dp_of(z, (x + k) % 4, c), y)
        if axis == "z":
            return (dp_of((z + k) % 4, x, c), y)
        return (dp, (y + k) % 4)

    def chunk(ref, lead, dims, axis, at):
        pos = dims.index(axis)
        return ref.at[tuple(lead) + (slice(None),) * pos + (at,)]

    def scatter(source, landing, lead, dims, axis, send, sem):
        for k in range(1, 4):
            at = (sizes[axis] + k) % 4
            launch(
                remote(
                    chunk(source, lead, dims, axis, at),
                    landing.at[tuple(lead) + (k - 1,)],
                    rs_s.at[send],
                    rs_r.at[sem],
                    peer(axis, k),
                )
            )

    def gather(source, landing, lead, dims, axis):
        total = chunk(source, lead, dims, axis, sizes[axis])[...].astype(F32)
        for k in range(3):
            total = total + landing[tuple(lead) + (k,)].astype(F32)
        return total

    def norm_back(upstream, gain, xhat, der, rstd, start, count, sums):
        dy = upstream * der[pl.ds(start, count), :]
        normal = xhat[pl.ds(start, count), :]
        dyn = dy * normal
        dg = sums[0] + dyn.reshape(count // 8, 8, 512).sum(axis=0)
        ds = sums[1] + dy.reshape(count // 8, 8, 512).sum(axis=0)
        mean_d = jnp.mean(dy * gain, axis=-1, keepdims=True)
        mean_dn = jnp.mean(dyn * gain, axis=-1, keepdims=True)
        inv = rstd[pl.ds(start, count), :][:, 0:1]
        return inv * (dy * gain - mean_d - normal * mean_dn), (dg, ds)

    def put_norm(layer, sums):
        for half in range(2):
            row = sums[half].sum(axis=0, keepdims=True)
            for j in range(4):
                nrm[layer * 8 + half * 4 + j : layer * 8 + half * 4 + j + 1, :] = row[:, j * LANE : (j + 1) * LANE]

    zeros = (jnp.zeros((8, 512), F32), jnp.zeros((8, 512), F32))

    def second_body(i, sums):
        for h in range(2):
            start = pl.multiple_of(i * 64 + h * 32, 32)
            out, sums = norm_back(gh[pl.ds(start, 32), :], gain1, xhat1, der1, rstd1, start, 32, sums)
            gf[pl.ds(start, 32), :] = out.astype(BF)
        return sums

    sums1 = lax.fori_loop(0, 4, second_body, zeros)
    put_norm(1, sums1)
    grad_second = gf[pl.ds(0, 256), :]
    for h in range(2):
        gh[pl.ds(h * 256, 256), :] = dot(grad_second, wv[1, pl.ds(h * 512, 512), :], NT).astype(BF).astype(F32)

    def forward_frames():
        await_bytes(frecv.at[low, down], fg_r.at[0])
        launch(remote(frecv.at[low, down], frecv.at[low, down], fg_s.at[1], fg_r.at[2], (dp, up)))
        await_bytes(frecv.at[high, up], fg_r.at[1])
        launch(remote(frecv.at[high, up], frecv.at[high, up], fg_s.at[1], fg_r.at[2], (dp, down)))
        sent(frecv.at[:, y], fg_s.at[1])

    def kernel_grad(layer, left):
        for half in range(2):
            right = gf[0 : left.shape[1], half * 256 : half * 256 + 256]
            for h in range(4):
                part = dot(left[h * 256 : (h + 1) * 256, :], right).astype(BF)
                for j in range(2):
                    convp[layer, 2 * half + j, h] = part[:, j * LANE : (j + 1) * LANE].reshape(4, 2, 4, 8, LANE)
            for j in (2 * half, 2 * half + 1):
                launch(remote(convp.at[layer, j, :, :, 1 - c], convr.at[layer, j], rs_s.at[layer], rs_r.at[2 * layer + half], mate))
        sent(convr.at[layer], rs_s.at[layer])

    kernel_grad(1, hidt)
    forward_frames()

    def conv_core(layer, j):
        if j % 2 == 0:
            await_bytes(convr.at[layer, pl.ds(j, 2)], rs_r.at[2 * layer + j // 2])
        convb[layer, j] = (
            convp[layer, j, :, :, c].astype(F32) + convr[layer, j].astype(F32)
        ).astype(BF)

    base = ("z", "x", "y")
    plane = sorted([(i, j) for i in range(4) for j in range(4) if i or j], key=lambda one: one.count(2) * 5 + 4 - one.count(0), reverse=True)

    conv_axis = (("x", "z", "y", "y"), ("x", "z", "x", "z"))
    groups = {
        axis: [(layer, j) for layer in range(2) for j in range(4) if conv_axis[layer][j] == axis] for axis in "xyz"
    }
    order = "xyz"

    def others_of(axis):
        return tuple(one for one in base if one != axis)

    def conv_send(layer, j):
        scatter(convb, conv1, (layer, j), base, conv_axis[layer][j], 3 + layer, 5 if layer else 6 + j)
        if j == 3:
            sent(conv1.at[layer], rs_s.at[3 + layer])

    def conv_take(layer, j):
        axis = conv_axis[layer][j]
        if layer == 0:
            await_bytes(conv1.at[layer, j], rs_r.at[6 + j])
        elif j == 0:
            await_bytes(conv1.at[layer], rs_r.at[5])
        total = gather(convb, conv1, (layer, j), base, axis)
        convb1[order.index(axis), :, :, groups[axis].index((layer, j))] = total.astype(BF)

    def plane_peer(first, second, i, j):
        at = dict(sizes)
        at[first] = (at[first] + i) % 4
        at[second] = (at[second] + j) % 4
        return (dp_of(at["z"], at["x"], c), at["y"])

    def conv_last_send(axis):
        p, count = order.index(axis), len(groups[axis])
        first, second = others_of(axis)
        for n, (i, j) in enumerate(plane):
            launch(
                remote(
                    convb1.at[p, (sizes[first] + i) % 4, (sizes[second] + j) % 4, pl.ds(0, count)],
                    conv2.at[p, n, pl.ds(0, count)],
                    pl_s.at[p],
                    pl_r.at[p],
                    plane_peer(first, second, i, j),
                )
            )
        sent(conv2.at[p, :, pl.ds(0, count)], pl_s.at[p])

    def conv_last_take(axis):
        p, count = order.index(axis), len(groups[axis])
        first, second = others_of(axis)
        await_bytes(conv2.at[p, :, pl.ds(0, count)], pl_r.at[p])
        total = convb1[p, sizes[first], sizes[second], 0:count].astype(F32)
        for n in range(15):
            total = total + conv2[p, n, 0:count].astype(F32)
        for at, (layer, j) in enumerate(groups[axis]):
            gconv_out[layer, :, j * LANE : (j + 1) * LANE] = total[at]

    def first_body(i, sums):
        for h in range(2):
            start = pl.multiple_of(i * 64 + h * 32, 32)
            out, sums = norm_back(gh[pl.ds(start, 32), :], gain0, xhat0, der0, rstd0, start, 32, sums)
            gf[pl.ds(start, 32), :] = out.astype(BF)
        return sums

    sums0 = lax.fori_loop(0, 8, first_body, zeros)
    put_norm(0, sums0)
    to_mate = remote(nrm, nrmr, nm_s.at[0], nm_r.at[0], mate)
    to_mate.start()

    for j in range(4):
        conv_core(1, j)
        conv_send(1, j)
    kernel_grad(0, actt)
    for h in range(2):
        gx[pl.ds(h * 256, 256), :] = dot(gf[pl.ds(h * 256, 256), :], wv[0], NT)
    await_bytes(nrmr, nm_r.at[0])
    to_mate.wait_send()
    nrm[...] = nrm[...] + nrmr[...]
    for k in range(1, 4):
        launch(remote(nrm, nrm1.at[k - 1], nm_s.at[1], nm_r.at[1], peer("x", k)))
    for j in range(4):
        conv_core(0, j)
        conv_send(0, j)

    @pl.loop(0, 8)
    def _(i):
        for h in range(2):
            rows = gx[pl.ds(pl.multiple_of(h * 256 + i * 32, 32), 32), :]
            for k in range(2):
                for j in range(4):
                    xo[j, pl.ds(2 * h + k, 32, stride=4), :] = rows[:, k * 512 + j * LANE : k * 512 + (j + 1) * LANE]
        out = jnp.concatenate([xo[j] for j in range(4)], axis=1)
        gfeat_out[pl.ds(pl.multiple_of(i * 128, 128), 128), :] = out.astype(BF)

    await_bytes(frecv.at[low], fg_r.at[2])
    packin[...] = dot(frecv[...].reshape(1024, 512), query[...], TN).astype(BF)
    part = dot(packin[...], gpv[...], NT).astype(BF)
    projp[...] = part.reshape(4, 4, 2, 16, WIDE)
    launch(remote(projp.at[:, :, 1 - c], projr, rs_s.at[2], rs_r.at[4], mate))
    sent(projr, rs_s.at[2])
    packed_out[...] = dot(pall[mine[0], pl.ds(mine[1], 320), :], packin[...]).astype(BF)
    await_bytes(projr, rs_r.at[4])
    projb[...] = (projp[:, :, c].astype(F32) + projr[...].astype(F32)).astype(BF)
    for n, (i, j) in enumerate(plane):
        launch(
            remote(
                projb.at[(z + i) % 4, (x + j) % 4], proj1.at[n], pl_s.at[4], pl_r.at[4], plane_peer("z", "x", i, j)
            )
        )
    sent(proj1, pl_s.at[4])
    await_bytes(nrm1, nm_r.at[1])
    await_bytes(nrm1, nm_s.at[1])
    nrm[...] = nrm[...] + nrm1[0] + nrm1[1] + nrm1[2]
    for n, (i, j) in enumerate(plane):
        launch(remote(nrm, nrm2.at[n], pl_s.at[3], pl_r.at[3], plane_peer("z", "y", i, j)))
    sent(nrm2, pl_s.at[3])
    for j in range(4):
        conv_take(1, j)
    for axis in "xzy":
        for j in range(4):
            if conv_axis[0][j] == axis:
                conv_take(0, j)
        conv_last_send(axis)
    await_bytes(nrm2, pl_r.at[3])
    total = nrm[...]
    for n in range(15):
        total = total + nrm2[n]
    gnorm_out[...] = total
    await_bytes(proj1, pl_r.at[4])
    total = projb[z, x].astype(F32)
    for n in range(15):
        total = total + proj1[n].astype(F32)
    gproj_out[...] = total[:, 0:320]
    for axis in "xzy":
        conv_last_take(axis)

    for ref, sem in sends:
        await_bytes(ref, sem)

    @pl.when(odd == c)
    def _():
        await_bytes(gsendb.at[pl.ds(0, 63)], g_s.at[0])
        await_bytes(gsends, g_s.at[1])

    @pl.when(odd != c)
    def _():
        await_bytes(gsendb, g_s.at[0])
        await_bytes(gsends.at[pl.ds(0, 63)], g_s.at[1])

    await_bytes(fsend.at[pl.ds(0, 31)], a2a_s.at[0])


def finish(
    packed_in, gfeat_in, gconv_in, gproj_in, gnorm_in, packed_out, gfeat_out, gconv_out, gproj_out, gnorm_out, rows, sem
):
    copies = [
        pltpu.make_async_copy(packed_in, packed_out, sem.at[0]),
        pltpu.make_async_copy(gfeat_in, gfeat_out, sem.at[1]),
        pltpu.make_async_copy(gconv_in, gconv_out, sem.at[2]),
        pltpu.make_async_copy(gproj_in, gproj_out, sem.at[3]),
    ]
    for one in (1, 0, 2, 3):
        copies[one].start()
    d = lax.axis_index("dp") * 4 + lax.axis_index("mp")
    for layer in range(2):
        row = gnorm_in[pl.ds(layer * 8 + d // 16, 1), :]
        turned = pltpu.roll(row, LANE - (d % 16) * 8, 1)
        rows[layer : layer + 1, :] = turned[:, 0:8]
    copies.append(pltpu.make_async_copy(rows, gnorm_out, sem.at[4]))
    copies[-1].start()
    for one in copies:
        one.wait()


def local(features, lengths, dests, offsets, conv_weight, norm_gain, norm_shift, proj_weight, grad_packed):
    vmem = pl.BlockSpec(memory_space=pltpu.VMEM)
    hbm = pl.BlockSpec(memory_space=pltpu.HBM)
    S = pltpu.SMEM
    V = pltpu.VMEM
    D = pltpu.SemaphoreType.DMA
    scratch = [
        S((32,), jnp.int32), S((32,), jnp.int32), S((32,), jnp.int32), V((2, 512), F32), V((2, 512), F32),
        V((1024, 512), BF), V((2, 1024, 512), BF), V((WIDE, 512), BF), V((WIDE, 512), BF), V((4, 128, LANE), F32),
        V((512, 1024), BF), V((1024, 512), BF), V((256, 256), BF), V((512, 512), F32), V((512, 512), F32), V((512, 512), F32), V((512, LANE), F32),
        V((256, 512), F32), V((256, 512), F32), V((256, LANE), F32),
        V((256, 1024), BF), V((1024, 256), BF), V((256, 512), BF),
        V((4, 4, 8, 1, LANE), F32), V((1024, 512), BF), V((64, 8, 384), BF), V((64, 8, 256), BF), V((2, 32, 8, 384), BF), V((2, 32, 8, 256), BF),
        V((32, 8, 512), BF), V((32, 4, 8, 512), BF), V((2, 640, 512), BF), V((512, 512), BF),
        V((512, 512), F32), V((512, 512), BF), V((512, 1024), F32), V((4, 128, LANE), F32),
        V((2, 4, 4, 4, 2, 4, 8, LANE), BF), V((2, 4, 4, 4, 4, 8, LANE), BF), V((2, 4, 4, 4, 4, 8, LANE), BF),
        V((2, 4, 3, 4, 4, 8, LANE), BF), V((3, 4, 4, 3, 8, LANE), BF), V((3, 15, 3, 8, LANE), BF),
        V((4, 4, 2, 16, WIDE), BF), V((4, 4, 16, WIDE), BF), V((4, 4, 16, WIDE), BF), V((15, 16, WIDE), BF),
        V((16, LANE), F32), V((16, LANE), F32), V((3, 16, LANE), F32), V((15, 16, LANE), F32),
        D((10,)), D((3,)), D((3,)), D((4,)), D((5,)), D((2,)), D((2,)), D((1,)), D((1,)), D((2,)), D((3,)), D((5,)), D((10,)),
        D((2,)), D((2,)), D((5,)), D((5,)),
    ]
    results = ((320, 512), BF), ((1024, 512), BF), ((2, 8, 512), F32), ((16, 320), F32), ((16, LANE), F32)
    middle = pl.pallas_call(
        kernel,
        out_shape=tuple(pltpu.VMEM(*one) for one in results),
        in_specs=[hbm] * 9,
        out_specs=(vmem,) * 5,
        scratch_shapes=scratch,
        compiler_params=pltpu.CompilerParams(collective_id=0, has_side_effects=True, vmem_limit_bytes=65_400_000),
    )(
        lengths, dests, offsets, norm_gain, norm_shift, features.reshape(1024, 512), conv_weight,
        proj_weight.T, grad_packed.T,
    )
    shapes = (*results[:4], ((2, 8), F32))
    packed, gfeat, gconv, gproj, gnorm = pl.pallas_call(
        finish,
        out_shape=tuple(jax.ShapeDtypeStruct(*one) for one in shapes),
        in_specs=[vmem] * 5,
        out_specs=(hbm,) * 5,
        scratch_shapes=[V((2, 8), F32), D((5,))],
    )(*[pltpu.with_memory_space_constraint(one, pltpu.VMEM) for one in middle])
    return packed.T, gfeat.reshape(32, 32, 512), gconv, gnorm, gproj


def solution(mesh):
    return jax.shard_map(
        local,
        mesh=mesh,
        in_specs=(
            P(("dp", "mp"), None, None),
            P(("dp", "mp")),
            P(("dp", "mp")),
            P(("dp", "mp")),
            P(),
            P(),
            P(),
            P(None, "mp"),
            P("dp", "mp"),
        ),
        out_specs=(
            P("dp", "mp"),
            P(("dp", "mp"), None, None),
            P(None, ("dp", "mp"), None),
            P(None, ("dp", "mp")),
            P("dp", "mp"),
        ),
        check_vma=False,
    )
```
